256 devices in a mesh: row: 8 (over x, z_hi), col: 32 (over y, z_lo, core).
Axes of the slice: x: 4, y: 4, z: 8 (z_hi: 2, z_lo: 4; z = z_hi * 4 + z_lo), core: 2. Of those that a mesh axis runs over, the one named last changes fastest.
Arguments:
- matrix: float32 [16384, 16384], P('row', 'col'), may hold values from -6 to 6, as said below
- vectors: float32 [2, 16384, 128], P(None, ('row', 'col')), may hold values from -0.16 to 0.16
- tfactor: float32 [2, 128, 128], replicated, may hold values from -0.5 to 0.5
Outputs:
- updated: float32 [16384, 16384], P('row', 'col')
The draws below stay inside these ranges and needn't reach their ends.
Inputs may be any that keep to these rules, and one draw needn't show every extreme that they name: matrix is symmetric: matrix[i, j] equals matrix[j, i].
All inputs are finite; a program needn't handle non-finite values.
Results may differ from the reference program's by a relative error of at most 0.00012.
Values sent between devices are 32-bit elements; how exact they have to be, the bound alone decides.
A program may use at most 64 MiB of HBM per device.

```python
import jax
import jax.numpy as jnp
from jax import lax

NA = 16384
B = 128
PANELS = 2


def draw_matrix(key, part):
    first = jax.random.fold_in(key, 7101)
    noise = jax.random.normal(first, (NA, NA), jnp.float32)
    sym = (noise + noise.T) * 0.7071
    sym = jnp.clip(sym, -6.0, 6.0)
    sym = sym.at[0, NA - 1].set(6.0).at[NA - 1, 0].set(6.0)
    sym = sym.at[1, 2].set(-6.0).at[2, 1].set(-6.0)
    return sym.astype(jnp.float32)


def block_levels(own_key, dims, pieces, low, top_value):
    def one(dim, shards_of):
        heights = jax.random.uniform(jax.random.fold_in(jax.random.fold_in(own_key, 6), dim), (shards_of,), jnp.float32, low / len(pieces), top_value / len(pieces))
        return jnp.repeat(jnp.exp(heights), dims[dim] // shards_of).reshape((-1,) + (1,) * (len(dims) - dim - 1))

    loudness = one(*pieces[0])
    for cut in pieces[1:]:
        loudness = loudness * one(*cut)
    return loudness


def normal_values(key, shape, spread, most, pieces=(), kind=jnp.bfloat16):
    gain = block_levels(key, shape, pieces, -0.22, 0.18) if pieces else 1.0
    drawn = jax.random.normal(key, shape, jnp.float32) * spread * gain
    return jnp.minimum(jnp.maximum(drawn, -most), most).astype(kind)


def setup_inputs(seed: int = 0) -> dict:
    key_list = jax.random.split(jax.random.key(seed), 4)
    matrix = draw_matrix(jax.random.fold_in(key_list[3], 71), 0)
    vectors = normal_values(key_list[1], (PANELS, NA, B), (0.026 + 0.1 * min(1, 16384 // NA // 64)), 0.16, ((1, 256),), jnp.float32)
    tfactor = normal_values(key_list[2], (PANELS, B, B), B ** -0.5, 0.5, (), jnp.float32)
    return {"matrix": matrix, "vectors": vectors, "tfactor": tfactor}


highest = lax.Precision.HIGHEST


def mat_product(left, right):
    return jnp.dot(left, right, precision=highest, preferred_element_type=jnp.float32)


def reference(matrix, vectors, tfactor):
    current = matrix
    for panel_index in range(PANELS):
        vector = vectors[panel_index]
        factor = jnp.triu(tfactor[panel_index])
        product = mat_product(current, vector)
        ymatrix = mat_product(product, factor)
        gram_matrix = mat_product(vector.T, ymatrix)
        wmatrix = ymatrix - 0.5 * mat_product(vector, mat_product(factor.T, gram_matrix))
        blocks = current.reshape(8, NA // 8, NA)
        v_blocks = vector.reshape(8, NA // 8, B)
        w_blocks = wmatrix.reshape(8, NA // 8, B)

        def update(members, vector=vector, wmatrix=wmatrix):
            row_block, v_rows, w_rows = members
            return row_block - mat_product(v_rows, wmatrix.T) - mat_product(w_rows, vector.T)

        current = lax.map(update, (blocks, v_blocks, w_blocks)).reshape(NA, NA)
    return current
```

```python
import jax
import jax.numpy as jnp
from jax import lax
from jax.experimental import pallas as pl
from jax.experimental.pallas import tpu as pltpu
from jax.sharding import PartitionSpec as P

MESH = pl.DeviceIdType.MESH
F32 = jnp.float32
BF16 = jnp.bfloat16
NN = ((1,), (0,))
TN = ((0,), (0,))


def split(value):
    high = value.astype(BF16)
    return high, (value - high.astype(F32)).astype(BF16)


def dot3(left, right, dims=NN):
    (lh, ll), (rh, rl) = left, right

    def one(a, b):
        return lax.dot_general(a, b, (dims, ((), ())), preferred_element_type=F32)

    return one(lh, rh) + (one(lh, rl) + one(ll, rh))


def dot_full(left, right):
    return jnp.dot(
        left, right, precision=lax.Precision.HIGHEST, preferred_element_type=F32
    )


def exchange_kernel(
    mat, vec, tf, vi_out, pi_out, xh_out, xl_out,
    a, vi, pi, vj, pj, part, ra, rb, ta, tb, fam, fap, fbp, fbm, total, l1,
    s1, s32, s2, s8, s3, sfull,
    send_sem, load_sem, zr, yr, cr, l2r, xr, rsr, l1r, s1r, s2r, s3r, s4r, s5r, s6r, out_sem,
):
    row, col = lax.axis_index("row"), lax.axis_index("col")
    x, zh = lax.div(row, 2), lax.rem(row, 2)
    y, zl, c = lax.div(col, 8), lax.rem(lax.div(col, 2), 4), lax.rem(col, 2)

    def mod4(v):
        return lax.rem(v + 8, 4)

    def dev(x_, zh_, y_, zl_, c_):
        return (x_ * 2 + zh_, (y_ * 4 + zl_) * 2 + c_)

    partner = dev(x, zh, y, zl, 1 - c)

    def at_x(k):
        return dev(mod4(x + k), zh, y, zl, c)

    def at_y(k):
        return dev(x, zh, mod4(y + k), zl, c)

    def at_zl(k):
        return dev(x, zh, y, mod4(zl + k), c)

    def at_z(k):
        z = lax.rem(zh * 4 + zl + k, 8)
        return dev(x, lax.div(z, 4), y, lax.rem(z, 4), c)

    def spread_to(h):
        return dev(zl, h, x, 2 * zh + lax.div(y, 2), lax.rem(y, 2))

    def owner(c_):
        return dev(y, lax.div(zl, 2), lax.rem(zl, 2) * 2 + c, x, c_)

    def is_me(d):
        return jnp.logical_and(d[0] == row, d[1] == col)

    def rows(ref, start, count):
        return ref.at[pl.ds(pl.multiple_of(start, 8), count)]

    def blk(ref, y_, zl_, c_):
        return rows(ref, ((y_ * 4 + zl_) * 2 + c_) * 64, 64)

    sent = []

    def send(src, dst, sem, device):
        copy = pltpu.make_async_remote_copy(
            src_ref=src, dst_ref=dst, send_sem=send_sem.at[len(sent)], recv_sem=sem,
            device_id=device, device_id_type=MESH,
        )
        copy.start()
        sent.append((copy, None))

    def send_or_keep(src, dst, sem, device):
        mine = is_me(device)
        copy = pltpu.make_async_remote_copy(
            src_ref=src, dst_ref=dst, send_sem=send_sem.at[len(sent)], recv_sem=sem,
            device_id=device, device_id_type=MESH,
        )
        keep = pltpu.make_async_copy(src, dst, sem)

        @pl.when(mine)
        def _():
            keep.start()

        @pl.when(jnp.logical_not(mine))
        def _():
            copy.start()

        sent.append((copy, jnp.logical_not(mine)))

    def arrived(dst, sem):
        pltpu.make_async_copy(dst, dst, sem).wait()

    load_a = pltpu.make_async_copy(mat, a, load_sem.at[0])
    own_v = blk(vi, y, zl, c)
    load_v = [
        pltpu.make_async_copy(
            vec.at[p],
            vi.at[pl.ds(pl.multiple_of(col * 64, 8), 64), pl.ds(128 * p, 128)],
            load_sem.at[1 + p],
        )
        for p in range(2)
    ]
    for copy in load_v:
        copy.start()
    load_a.start()

    barrier = pltpu.get_barrier_semaphore()
    peers = [partner] + [at_x(k) for k in (1, 2, 3)] + [at_y(k) for k in (1, 2, 3)]
    peers += [at_z(k) for k in range(1, 8)]
    for peer in peers:
        pl.semaphore_signal(barrier, inc=1, device_id=peer, device_id_type=MESH)
    for peer in (spread_to(0), spread_to(1), owner(0), owner(1)):

        @pl.when(jnp.logical_not(is_me(peer)))
        def _(peer=peer):
            pl.semaphore_signal(barrier, inc=1, device_id=peer, device_id_type=MESH)

    for copy in load_v:
        copy.wait()
    fixed = jnp.logical_or(is_me(spread_to(0)), is_me(spread_to(1)))
    pl.semaphore_wait(barrier, len(peers) + 4 - 2 * fixed.astype(jnp.int32))

    zk = [mod4(zl - k) for k in range(4)]
    yn = [y, mod4(y - 1), mod4(y + 1), mod4(y + 2)]

    def half(ref, y_, zl_, c_, h):
        return rows(ref, ((y_ * 4 + zl_) * 2 + c_) * 64 + 32 * h, 32)

    class Spread:
        def __init__(self, n, big, small):
            self.n, self.big, self.small = n, big, small

        def to_partner(self, n, k):
            b = blk(self.big, yn[n], zk[k], c)
            send(b, b, cr.at[self.n, n, k], partner)

        def to_y(self, k):
            b = blk(self.big, y, zk[k], c)
            send(b, b, yr.at[self.n, k, 0], at_y(1))
            send(b, b, yr.at[self.n, k, 1], at_y(3))

        def start(self):
            b = blk(self.big, y, zl, c)
            for k in (1, 2, 3):
                send(b, b, zr.at[self.n, k - 1], at_zl(k))
            self.to_y(0)
            self.to_partner(0, 0)
            d = rows(self.small, (2 * zl + c) * 64, 64)
            for h in range(2):
                send_or_keep(b, d, l2r.at[self.n, c], spread_to(h))

        def z_step(self):
            for k in (1, 2, 3):
                arrived(blk(self.big, y, zk[k], c), zr.at[self.n, k - 1])
                self.to_y(k)
                self.to_partner(0, k)

        def y_step(self, k):
            arrived(blk(self.big, yn[1], zk[k], c), yr.at[self.n, k, 0])
            h = half(self.big, yn[1], zk[k], c, 0)
            send(h, h, yr.at[self.n, k, 2], at_y(1))
            self.to_partner(1, k)
            arrived(blk(self.big, yn[2], zk[k], c), yr.at[self.n, k, 1])
            h = half(self.big, yn[2], zk[k], c, 1)
            send(h, h, yr.at[self.n, k, 3], at_y(3))
            self.to_partner(2, k)

        def y_last(self, k):
            for h in range(2):
                arrived(half(self.big, yn[3], zk[k], c, h), yr.at[self.n, k, 2 + h])
            self.to_partner(3, k)

        def from_partner(self, n):
            for k in range(4):
                arrived(blk(self.big, yn[n], zk[k], 1 - c), cr.at[self.n, n, k])

        def x_start(self):
            for h in range(2):
                arrived(rows(self.small, (2 * x + h) * 64, 64), l2r.at[self.n, h])
            b = rows(self.small, x * 128, 128)
            send(b, b, xr.at[self.n, 0], at_x(1))
            send(b, b, xr.at[self.n, 1], at_x(3))

        def x_step(self):
            m = mod4(x - 1)
            arrived(rows(self.small, m * 128, 128), xr.at[self.n, 0])
            h = rows(self.small, m * 128, 64)
            send(h, h, xr.at[self.n, 2], at_x(1))
            m = mod4(x + 1)
            arrived(rows(self.small, m * 128, 128), xr.at[self.n, 1])
            h = rows(self.small, m * 128 + 64, 64)
            send(h, h, xr.at[self.n, 3], at_x(3))

        def x_last(self):
            m = mod4(x + 2)
            for h in range(2):
                arrived(rows(self.small, m * 128 + 64 * h, 64), xr.at[self.n, 2 + h])

    sv = Spread(0, vi, vj)
    sv.start()
    sv.z_step()
    sv.x_start()
    for k in range(4):
        sv.y_step(k)
    sv.x_step()
    load_a.wait()

    def chunk(n):
        start = pl.multiple_of(yn[n] * 512, 512)
        vt = vi[pl.ds(start, 512), :].T
        return dot3(split(vt), split(a[pl.ds(start, 512), :]))

    sv.from_partner(0)
    pt = chunk(0)
    for k in range(4):
        sv.y_last(k)
    sv.from_partner(1)
    pt += chunk(1)
    sv.from_partner(2)
    pt += chunk(2)
    sv.x_last()
    sv.from_partner(3)
    pt += chunk(3)
    out_v = pltpu.make_async_copy(vi, vi_out, out_sem.at[0])
    out_v.start()

    pfull = pt.T
    for q in range(4):
        part[192 * q : 192 * q + 128, :] = pfull[128 * q : 128 * q + 128, :]
    s_part = dot3(split(vj[...].T), split(pfull))
    own = own_v[...]
    n_part = dot3(split(own[:, :128].T), split(own[:, 128:]))
    for q in range(2):
        part[192 * q + 128 : 192 * q + 192, :] = s_part[64 * q : 64 * q + 64, :]
    for q in range(2):
        low = slice(192 * (q + 2) + 128, 192 * (q + 2) + 192)
        part[low, :128] = n_part[64 * q : 64 * q + 64, :]
        part[low, 128:] = s_part[128 + 64 * q : 192 + 64 * q, 128:]

    def piece(k, h):
        return rows(part, mod4(x + k) * 192 + 96 * h, 96)

    send(piece(2, 0), ra, rsr.at[0], at_x(1))
    send(piece(2, 1), rb, rsr.at[1], at_x(3))
    send(piece(1, 1), fbm, rsr.at[2], at_x(1))
    send(piece(3, 0), fap, rsr.at[3], at_x(3))
    arrived(ra, rsr.at[0])
    ta[...] = ra[...] + piece(1, 0)[...]
    send(ta, fam, rsr.at[4], at_x(1))
    arrived(rb, rsr.at[1])
    tb[...] = rb[...] + piece(3, 1)[...]
    send(tb, fbp, rsr.at[5], at_x(3))
    arrived(fap, rsr.at[3])
    arrived(fbm, rsr.at[2])
    arrived(fam, rsr.at[4])
    total[0:96, :] = piece(0, 0)[...] + (fam[...] + fap[...])
    arrived(fbp, rsr.at[5])
    total[96:192, :] = piece(0, 1)[...] + (fbp[...] + fbm[...])

    for h in range(2):
        send_or_keep(total.at[pl.ds(64 * h, 64)], l1.at[zh], l1r.at[zh], owner(h))
    send(rows(total, 128 + 32 * (1 - c), 32), s1, s1r, partner)
    arrived(s1, s1r)
    s32[...] = rows(total, 128 + 32 * c, 32)[...] + s1[...]
    for k in (1, 2, 3):
        send(rows(s32, 8 * mod4(y + k), 8), s2.at[k - 1], s2r.at[k - 1], at_y(k))
    for h in range(2):
        arrived(l1.at[h], l1r.at[h])
    blk(pi, y, zl, c)[...] = l1[0] + l1[1]
    sp = Spread(1, pi, pj)
    sp.start()
    for k in range(3):
        arrived(s2.at[k], s2r.at[k])
    s8[...] = rows(s32, 8 * y, 8)[...] + s2[0] + (s2[1] + s2[2])
    for k in range(1, 8):
        send(s8, s3.at[k - 1], s3r.at[k - 1], at_z(k))
    sp.z_step()
    for k in range(7):
        arrived(s3.at[k], s3r.at[k])
    mine = s8[...] + s3[0] + (s3[1] + s3[2]) + ((s3[3] + s3[4]) + (s3[5] + s3[6]))

    def srow(x_, y_, c_):
        return rows(sfull, 64 * x_ + 32 * c_ + 8 * y_, 8)

    srow(x, y, c)[...] = mine
    for k in (1, 2, 3):
        send(srow(x, y, c), srow(x, y, c), s4r.at[k - 1], at_y(k))
    sp.x_start()
    sp.y_step(0)
    sp.y_step(1)
    for k in (1, 2, 3):
        arrived(srow(x, mod4(y - k), c), s4r.at[k - 1])
    s_own = rows(sfull, 64 * x + 32 * c, 32)
    for k in (1, 2, 3):
        send(s_own, s_own, s5r.at[k - 1], at_x(k))
    send(s_own, s_own, s6r.at[0], partner)
    sp.y_step(2)
    sp.y_step(3)
    sp.x_step()
    for k in (1, 2, 3):
        s_k = rows(sfull, 64 * mod4(x - k) + 32 * c, 32)
        arrived(s_k, s5r.at[k - 1])
        send(s_k, s_k, s6r.at[k], partner)
    for k in range(4):
        sp.y_last(k)
    for k in range(4):
        arrived(rows(sfull, 64 * mod4(x - k) + 32 * (1 - c), 32), s6r.at[k])

    upper = lax.broadcasted_iota(jnp.int32, (128, 128), 0) <= lax.broadcasted_iota(
        jnp.int32, (128, 128), 1
    )
    t1 = jnp.where(upper, tf[0], 0.0)
    t2 = jnp.where(upper, tf[1], 0.0)
    s11, s12 = sfull[0:128, 0:128], sfull[0:128, 128:256]
    n12, s22 = sfull[128:256, 0:128], sfull[128:256, 128:256]
    t1t, t2t = t1.T, t2.T
    b = dot_full(t1t, dot_full(s11, t1))
    e = dot_full(t1t, s12)
    h = dot_full(b.T, n12)
    nt2 = dot_full(n12, t2)
    f = dot_full(n12.T, e - 0.5 * h)
    k12 = dot_full(h - e, t2)
    m12 = -dot_full(t1, nt2)
    b2 = dot_full(t2t, dot_full(s22 - f - f.T, t2))
    zero = jnp.zeros((128, 128), F32)
    kk = jnp.concatenate(
        [
            jnp.concatenate([-0.5 * (b + b.T), k12], axis=1),
            jnp.concatenate([k12.T, -0.5 * (b2 + b2.T)], axis=1),
        ],
        axis=0,
    )
    mm = jnp.concatenate(
        [jnp.concatenate([t1, m12], axis=1), jnp.concatenate([zero, t2], axis=1)], axis=0
    )
    sp.x_last()
    m_s = split(mm)
    v_s = split(vj[...])
    xj = dot3(split(pj[...]), m_s) + dot3(v_s, split(kk))
    zj = dot3(v_s, split(mm.T))
    for n, value in enumerate((xj, zj)):
        high, low = split(value.T)
        xh_out[256 * n : 256 * n + 256, :] = high
        xl_out[256 * n : 256 * n + 256, :] = low

    for n in range(4):
        sp.from_partner(n)
    out_p = pltpu.make_async_copy(pi, pi_out, out_sem.at[1])
    out_p.start()
    for copy, when in sent:
        if when is None:
            copy.wait_send()
        else:

            @pl.when(when)
            def _(copy=copy):
                copy.wait_send()

    out_v.wait()
    out_p.wait()


def exchange(matrix, vectors, tfactor):
    def vmem(*shape):
        return pltpu.VMEM(shape, F32)

    def dma(*shape):
        return pltpu.SemaphoreType.DMA(shape)

    return pl.pallas_call(
        exchange_kernel,
        out_shape=(
            jax.ShapeDtypeStruct((2048, 256), F32),
            jax.ShapeDtypeStruct((2048, 256), F32),
            jax.ShapeDtypeStruct((512, 512), BF16),
            jax.ShapeDtypeStruct((512, 512), BF16),
        ),
        in_specs=[
            pl.BlockSpec(memory_space=pl.ANY),
            pl.BlockSpec(memory_space=pl.ANY),
            pl.BlockSpec(memory_space=pltpu.VMEM),
        ],
        out_specs=(
            pl.BlockSpec(memory_space=pl.ANY),
            pl.BlockSpec(memory_space=pl.ANY),
            pl.BlockSpec(memory_space=pltpu.VMEM),
            pl.BlockSpec(memory_space=pltpu.VMEM),
        ),
        scratch_shapes=[
            vmem(2048, 512), vmem(2048, 256), vmem(2048, 256), vmem(512, 256), vmem(512, 256),
            vmem(768, 256), vmem(96, 256), vmem(96, 256), vmem(96, 256), vmem(96, 256),
            vmem(96, 256), vmem(96, 256), vmem(96, 256), vmem(96, 256), vmem(192, 256),
            vmem(2, 64, 256), vmem(32, 256), vmem(32, 256), vmem(3, 8, 256), vmem(8, 256),
            vmem(7, 8, 256), vmem(256, 256),
            dma(160), dma(3), dma(2, 3), dma(2, 4, 4), dma(2, 4, 4), dma(2, 2), dma(2, 4),
            dma(6), dma(2), dma(), dma(3), dma(7), dma(3), dma(3), dma(4), dma(2),
        ],
        compiler_params=pltpu.CompilerParams(
            collective_id=0, has_side_effects=True, vmem_limit_bytes=48 << 20
        ),
    )(matrix, vectors, tfactor)


def update_kernel(mat, vi, pi, xh, xl, out):
    left = split(jnp.concatenate([vi[...], pi[...]], axis=1))
    out[...] = mat[...] - dot3(left, (xh[...], xl[...]))


def update(matrix, vi, pi, xh, xl):
    rows_here, cols_here = matrix.shape
    step = 512
    return pl.pallas_call(
        update_kernel,
        grid=(rows_here // step,),
        out_shape=jax.ShapeDtypeStruct(matrix.shape, F32),
        in_specs=[
            pl.BlockSpec((step, cols_here), lambda i: (i, 0)),
            pl.BlockSpec((step, 256), lambda i: (i, 0)),
            pl.BlockSpec((step, 256), lambda i: (i, 0)),
            pl.BlockSpec((512, 512), lambda i: (0, 0)),
            pl.BlockSpec((512, 512), lambda i: (0, 0)),
        ],
        out_specs=pl.BlockSpec((step, cols_here), lambda i: (i, 0)),
        compiler_params=pltpu.CompilerParams(vmem_limit_bytes=32 << 20),
    )(matrix, vi, pi, xh, xl)


def body(matrix, vectors, tfactor):
    return update(matrix, *exchange(matrix, vectors, tfactor))


def solution(mesh):
    return jax.shard_map(
        body,
        mesh=mesh,
        in_specs=(P("row", "col"), P(None, ("row", "col"), None), P()),
        out_specs=P("row", "col"),
        check_vma=False,
    )
```

```python
import jax
import jax.numpy as jnp
from jax import lax
from jax.experimental import pallas as pl
from jax.experimental.pallas import tpu as pltpu
from jax.sharding import PartitionSpec as P

MESH = pl.DeviceIdType.MESH
F32 = jnp.float32
BF16 = jnp.bfloat16
NN = ((1,), (0,))
TN = ((0,), (0,))


def split(value):
    high = value.astype(BF16)
    return high, (value - high.astype(F32)).astype(BF16)


def dot3(left, right, dims=NN):
    (lh, ll), (rh, rl) = left, right

    def one(a, b):
        return lax.dot_general(a, b, (dims, ((), ())), preferred_element_type=F32)

    return one(lh, rh) + (one(lh, rl) + one(ll, rh))


def dot_full(left, right):
    return jnp.dot(
        left, right, precision=lax.Precision.HIGHEST, preferred_element_type=F32
    )


def exchange_kernel(
    mat, vec, tf, a2, pi, zh_out, zl_out,
    a, vi, vj, pj, part, ra, rb, ta, tb, fam, fap, fbp, fbm, total, l1, hx,
    sp_, s1, s128, sx, s32, sy, s8, sz, sfull, tfv,
    send_sem, load_sem, zr, yr, cr, l2r, xr, rsr, l1r, hr, s1r, sxr, syr, szr, s4r, s5r, s6r,
):
    row, col = lax.axis_index("row"), lax.axis_index("col")
    x, zh = lax.div(row, 2), lax.rem(row, 2)
    y, zl, c = lax.div(col, 8), lax.rem(lax.div(col, 2), 4), lax.rem(col, 2)

    def mod4(v):
        return lax.rem(v + 8, 4)

    def dev(x_, zh_, y_, zl_, c_):
        return (x_ * 2 + zh_, (y_ * 4 + zl_) * 2 + c_)

    partner = dev(x, zh, y, zl, 1 - c)

    def at_x(k):
        return dev(mod4(x + k), zh, y, zl, c)

    def at_y(k):
        return dev(x, zh, mod4(y + k), zl, c)

    zk = [zl, zl + 1 - 2 * lax.rem(zl, 2), mod4(zl + 2), 3 - zl]
    yn = [y, mod4(y - 1), mod4(y + 1), mod4(y + 2)]

    def at_zl(k):
        return dev(x, zh, y, zk[k], c)

    def at_z(k):
        z = lax.rem(zh * 4 + zl + k, 8)
        return dev(x, lax.div(z, 4), y, lax.rem(z, 4), c)

    def spread_to(h):
        return dev(zl, h, x, 2 * zh + lax.div(y, 2), lax.rem(y, 2))

    def spread_from(h):
        return dev(y, lax.div(zl, 2), lax.rem(zl, 2) * 2 + c, x, h)

    def owner(h):
        return dev(y, lax.div(zl, 2), x, lax.rem(zl, 2) * 2 + c, h)

    def owned_from(h):
        return dev(y, h, x, 2 * zh + lax.div(zl, 2), lax.rem(zl, 2))

    def is_me(d):
        return jnp.logical_and(d[0] == row, d[1] == col)

    def rows(ref, start, count):
        return ref.at[pl.ds(pl.multiple_of(start, 8), count)]

    sent = []

    def send(src, dst, sem, device):
        copy = pltpu.make_async_remote_copy(
            src_ref=src, dst_ref=dst, send_sem=send_sem.at[len(sent)], recv_sem=sem,
            device_id=device, device_id_type=MESH,
        )
        copy.start()
        sent.append((copy, None))

    def send_or_keep(src, dst, sem, device):
        mine = is_me(device)
        copy = pltpu.make_async_remote_copy(
            src_ref=src, dst_ref=dst, send_sem=send_sem.at[len(sent)], recv_sem=sem,
            device_id=device, device_id_type=MESH,
        )
        keep = pltpu.make_async_copy(src, dst, sem)

        @pl.when(mine)
        def _():
            keep.start()

        @pl.when(jnp.logical_not(mine))
        def _():
            copy.start()

        sent.append((copy, jnp.logical_not(mine)))

    def finish():
        for copy, when in sent:
            if when is None:
                copy.wait_send()
            else:

                @pl.when(when)
                def _(copy=copy):
                    copy.wait_send()

    def arrived(dst, sem):
        pltpu.make_async_copy(dst, dst, sem).wait()

    load_a = pltpu.make_async_copy(mat, a, load_sem.at[0])
    load_t = pltpu.make_async_copy(tf, tfv, load_sem.at[3])
    load_v = [
        pltpu.make_async_copy(
            vec.at[p],
            vi.at[pl.ds(pl.multiple_of(col * 64, 8), 64), pl.ds(128 * p, 128)],
            load_sem.at[1 + p],
        )
        for p in range(2)
    ]
    for copy in load_v:
        copy.start()
    load_a.start()
    load_t.start()

    barrier = pltpu.get_barrier_semaphore()
    peers = [partner] + [at_x(k) for k in (1, 2, 3)] + [at_y(k) for k in (1, 2, 3)]
    peers += [at_z(k) for k in range(1, 8)]
    for peer in peers:
        pl.semaphore_signal(barrier, inc=1, device_id=peer, device_id_type=MESH)
    others = [f(h) for f in (spread_to, spread_from, owner, owned_from) for h in range(2)]
    for peer in others:

        @pl.when(jnp.logical_not(is_me(peer)))
        def _(peer=peer):
            pl.semaphore_signal(barrier, inc=1, device_id=peer, device_id_type=MESH)

    for copy in load_v:
        copy.wait()
    count = len(peers) + len(others)
    for peer in others:
        count = count - is_me(peer).astype(jnp.int32)
    pl.semaphore_wait(barrier, count)

    class Gather:
        def __init__(self, n, big, place):
            self.n, self.big, self.place = n, big, place

        def blk(self, y_, zl_, c_):
            return rows(self.big, self.place(y_, zl_, c_) * 64, 64)

        def half(self, y_, zl_, c_, h):
            return rows(self.big, self.place(y_, zl_, c_) * 64 + 32 * h, 32)

        def to_partner(self, n, k):
            b = self.blk(yn[n], zk[k], c)
            send(b, b, cr.at[self.n, n, k], partner)

        def to_y(self, k):
            b = self.blk(y, zk[k], c)
            send(b, b, yr.at[self.n, k, 0], at_y(1))
            send(b, b, yr.at[self.n, k, 1], at_y(3))

        def start(self):
            b = self.blk(y, zl, c)
            for k in (1, 2, 3):
                send(b, b, zr.at[self.n, k - 1], at_zl(k))
            self.to_y(0)
            self.to_partner(0, 0)

        def z_step(self, k):
            arrived(self.blk(y, zk[k], c), zr.at[self.n, k - 1])
            self.to_y(k)
            self.to_partner(0, k)

        def y_step(self, k):
            arrived(self.blk(yn[1], zk[k], c), yr.at[self.n, k, 0])
            h = self.half(yn[1], zk[k], c, 0)
            send(h, h, yr.at[self.n, k, 2], at_y(1))
            self.to_partner(1, k)
            arrived(self.blk(yn[2], zk[k], c), yr.at[self.n, k, 1])
            h = self.half(yn[2], zk[k], c, 1)
            send(h, h, yr.at[self.n, k, 3], at_y(3))
            self.to_partner(2, k)

        def y_last(self, k):
            for h in range(2):
                arrived(self.half(yn[3], zk[k], c, h), yr.at[self.n, k, 2 + h])
            self.to_partner(3, k)

        def from_partner(self, n):
            for k in range(4):
                arrived(self.blk(yn[n], zk[k], 1 - c), cr.at[self.n, n, k])

    class Ring:
        def __init__(self, n, small):
            self.n, self.small = n, small

        def start(self):
            b = rows(self.small, x * 128, 128)
            send(b, b, xr.at[self.n, 0], at_x(1))
            send(b, b, xr.at[self.n, 1], at_x(3))

        def step(self):
            m = mod4(x - 1)
            arrived(rows(self.small, m * 128, 128), xr.at[self.n, 0])
            h = rows(self.small, m * 128, 64)
            send(h, h, xr.at[self.n, 2], at_x(1))
            m = mod4(x + 1)
            arrived(rows(self.small, m * 128, 128), xr.at[self.n, 1])
            h = rows(self.small, m * 128 + 64, 64)
            send(h, h, xr.at[self.n, 3], at_x(3))

        def last(self):
            m = mod4(x + 2)
            for h in range(2):
                arrived(rows(self.small, m * 128 + 64 * h, 64), xr.at[self.n, 2 + h])

    gv = Gather(0, vi, lambda y_, zl_, c_: (y_ * 4 + zl_) * 2 + c_)
    rv = Ring(0, vj)
    gv.start()
    for h in range(2):
        send_or_keep(
            gv.blk(y, zl, c), rows(vj, (2 * zl + c) * 64, 64), l2r.at[c], spread_to(h)
        )
    for k in (1, 2, 3):
        gv.z_step(k)
    for k in range(3):
        gv.y_step(k)
    for h in range(2):
        arrived(rows(vj, (2 * x + h) * 64, 64), l2r.at[h])
    rv.start()
    gv.y_step(3)
    load_a.wait()
    load_t.wait()

    def chunk(n):
        start = pl.multiple_of(yn[n] * 512, 512)
        vt = vi[pl.ds(start, 512), :].T
        return dot3(split(vt), split(a[pl.ds(start, 512), :]))

    gv.from_partner(0)
    pt = chunk(0)
    rv.step()
    for k in range(4):
        gv.y_last(k)
    gv.from_partner(1)
    pt += chunk(1)
    gv.from_partner(2)
    pt += chunk(2)
    gv.from_partner(3)
    pt += chunk(3)
    part[...] = pt.T

    def piece(k, h):
        return rows(part, mod4(x + k) * 128 + 64 * h, 64)

    send(piece(2, 0), ra, rsr.at[0], at_x(1))
    send(piece(2, 1), rb, rsr.at[1], at_x(3))
    send(piece(1, 1), fbm, rsr.at[2], at_x(1))
    send(piece(3, 0), fap, rsr.at[3], at_x(3))

    rv.last()
    sp_[...] = dot3(split(vj[...].T), split(part[...]))
    own = gv.blk(y, zl, c)[...]
    sp_[128:256, 0:128] = dot3(split(own[:, :128].T), split(own[:, 128:]))
    send(rows(sp_, 128 * (1 - c), 128), s1, s1r, partner)
    arrived(s1, s1r)
    s128[...] = rows(sp_, 128 * c, 128)[...] + s1[...]
    for k in (1, 2, 3):
        send(rows(s128, 32 * mod4(x + k), 32), sx.at[k - 1], sxr.at[k - 1], at_x(k))

    arrived(ra, rsr.at[0])
    ta[...] = ra[...] + piece(1, 0)[...]
    send(ta, fam, rsr.at[4], at_x(1))
    arrived(rb, rsr.at[1])
    tb[...] = rb[...] + piece(3, 1)[...]
    send(tb, fbp, rsr.at[5], at_x(3))
    for k in range(3):
        arrived(sx.at[k], sxr.at[k])
    s32[...] = rows(s128, 32 * x, 32)[...] + sx[0] + (sx[1] + sx[2])
    for k in (1, 2, 3):
        send(rows(s32, 8 * mod4(y + k), 8), sy.at[k - 1], syr.at[k - 1], at_y(k))
    arrived(fap, rsr.at[3])
    arrived(fbm, rsr.at[2])
    arrived(fam, rsr.at[4])
    total[0:64, :] = piece(0, 0)[...] + (fam[...] + fap[...])
    send_or_keep(total.at[pl.ds(0, 64)], l1.at[zh], l1r.at[zh], owner(0))
    arrived(fbp, rsr.at[5])
    total[64:128, :] = piece(0, 1)[...] + (fbp[...] + fbm[...])
    send_or_keep(total.at[pl.ds(64, 64)], l1.at[zh], l1r.at[zh], owner(1))
    send(total, hx, hr, at_z(4))

    for k in range(3):
        arrived(sy.at[k], syr.at[k])
    s8[...] = rows(s32, 8 * y, 8)[...] + sy[0] + (sy[1] + sy[2])
    for k in range(1, 8):
        send(s8, sz.at[k - 1], szr.at[k - 1], at_z(k))
    arrived(hx, hr)
    rp = Ring(1, pj)
    rows(pj, x * 128, 128)[...] = total[...] + hx[...]
    rp.start()
    for h in range(2):
        arrived(l1.at[h], l1r.at[h])
    gp = Gather(1, pi, lambda y_, zl_, c_: (zl_ * 4 + y_) * 2 + c_)
    gp.blk(y, zl, c)[...] = l1[0] + l1[1]
    gp.start()

    def srow(x_, y_, c_):
        return rows(sfull, 128 * c_ + 32 * x_ + 8 * y_, 8)

    for k in range(7):
        arrived(sz.at[k], szr.at[k])
    srow(x, y, c)[...] = s8[...] + sz[0] + (sz[1] + sz[2]) + ((sz[3] + sz[4]) + (sz[5] + sz[6]))
    for k in (1, 2, 3):
        send(srow(x, y, c), srow(x, y, c), s4r.at[k - 1], at_y(k))
    gp.z_step(1)
    rp.step()
    for k in (1, 2, 3):
        arrived(srow(x, mod4(y - k), c), s4r.at[k - 1])
    s_own = rows(sfull, 128 * c + 32 * x, 32)
    for k in (1, 2, 3):
        send(s_own, s_own, s5r.at[k - 1], at_x(k))
    send(s_own, s_own, s6r.at[0], partner)
    gp.z_step(2)
    gp.z_step(3)
    gp.y_step(0)
    for k in (1, 2, 3):
        s_k = rows(sfull, 128 * c + 32 * mod4(x - k), 32)
        arrived(s_k, s5r.at[k - 1])
        send(s_k, s_k, s6r.at[k], partner)
    rp.last()
    gp.y_step(1)
    for k in range(4):
        arrived(rows(sfull, 128 * (1 - c) + 32 * mod4(x - k), 32), s6r.at[k])

    upper = lax.broadcasted_iota(jnp.int32, (128, 128), 0) <= lax.broadcasted_iota(
        jnp.int32, (128, 128), 1
    )
    t1 = jnp.where(upper, tfv[0], 0.0)
    t2 = jnp.where(upper, tfv[1], 0.0)
    s11, s12 = sfull[0:128, 0:128], sfull[0:128, 128:256]
    n12, s22 = sfull[128:256, 0:128], sfull[128:256, 128:256]
    t1t, t2t = t1.T, t2.T
    b = dot_full(t1t, dot_full(s11, t1))
    e = dot_full(t1t, s12)
    h = dot_full(b.T, n12)
    gp.y_step(2)
    nt2 = dot_full(n12, t2)
    f = dot_full(n12.T, e - 0.5 * h)
    k12 = dot_full(h - e, t2)
    m12 = -dot_full(t1, nt2)
    b2 = dot_full(t2t, dot_full(s22 - f - f.T, t2))
    gp.y_step(3)
    zero = jnp.zeros((128, 128), F32)
    kk = jnp.concatenate(
        [
            jnp.concatenate([-0.5 * (b + b.T), k12], axis=1),
            jnp.concatenate([k12.T, -0.5 * (b2 + b2.T)], axis=1),
        ],
        axis=0,
    )
    mm = jnp.concatenate(
        [jnp.concatenate([t1, m12], axis=1), jnp.concatenate([zero, t2], axis=1)], axis=0
    )
    v_s = split(vj[...])
    xj = dot3(split(pj[...]), split(mm)) + dot3(v_s, split(kk))
    zj = dot3(v_s, split(mm.T))
    zh_out[...], zl_out[...] = split(zj.T)
    x_s = split(xj.T)
    gp.y_last(0)
    gp.y_last(1)
    for n in range(4):
        r = slice(512 * n, 512 * n + 512)
        a2[r, :] = a[r, :] - dot3(split(vi[r, :]), x_s)
        if n == 0:
            gp.y_last(2)
            gp.y_last(3)
    for n in range(4):
        gp.from_partner(n)
    finish()


def exchange(matrix, vectors, tfactor):
    def vmem(*shape):
        return pltpu.VMEM(shape, F32)

    def dma(*shape):
        return pltpu.SemaphoreType.DMA(shape)

    return pl.pallas_call(
        exchange_kernel,
        out_shape=(
            jax.ShapeDtypeStruct((2048, 512), F32),
            jax.ShapeDtypeStruct((2048, 256), F32),
            jax.ShapeDtypeStruct((256, 512), BF16),
            jax.ShapeDtypeStruct((256, 512), BF16),
        ),
        in_specs=[pl.BlockSpec(memory_space=pltpu.HBM)] * 3,
        out_specs=(pl.BlockSpec(memory_space=pltpu.VMEM),) * 4,
        scratch_shapes=[
            vmem(2048, 512), vmem(2048, 256), vmem(512, 256), vmem(512, 256), vmem(512, 256),
            vmem(64, 256), vmem(64, 256), vmem(64, 256), vmem(64, 256),
            vmem(64, 256), vmem(64, 256), vmem(64, 256), vmem(64, 256), vmem(128, 256),
            vmem(2, 64, 256), vmem(128, 256),
            vmem(256, 256), vmem(128, 256), vmem(128, 256), vmem(3, 32, 256), vmem(32, 256),
            vmem(3, 8, 256), vmem(8, 256), vmem(7, 8, 256), vmem(256, 256), vmem(2, 128, 128),
            dma(160), dma(4), dma(2, 3), dma(2, 4, 4), dma(2, 4, 4), dma(2), dma(2, 4),
            dma(6), dma(2), dma(), dma(), dma(3), dma(3), dma(7), dma(3), dma(3), dma(4),
        ],
        compiler_params=pltpu.CompilerParams(
            collective_id=0, has_side_effects=True, vmem_limit_bytes=36 << 20
        ),
    )(*(pltpu.with_memory_space_constraint(v, pltpu.HBM) for v in (matrix, vectors, tfactor)))


def update_kernel(mat, pi, zh, zl, out):
    out[...] = mat[...] - dot3(split(pi[...]), (zh[...], zl[...]))


def update(matrix, pi, zh, zl):
    rows_here, cols_here = matrix.shape
    step = 512
    return pl.pallas_call(
        update_kernel,
        grid=(rows_here // step,),
        out_shape=jax.ShapeDtypeStruct(matrix.shape, F32),
        in_specs=[
            pl.BlockSpec((step, cols_here), lambda i: (i, 0)),
            pl.BlockSpec((step, 256), lambda i: (i, 0)),
            pl.BlockSpec((256, 512), lambda i: (0, 0)),
            pl.BlockSpec((256, 512), lambda i: (0, 0)),
        ],
        out_specs=pl.BlockSpec((step, cols_here), lambda i: (i, 0)),
        compiler_params=pltpu.CompilerParams(vmem_limit_bytes=20 << 20),
    )(matrix, pi, zh, zl)


def body(matrix, vectors, tfactor):
    return update(*exchange(matrix, vectors, tfactor))


def solution(mesh):
    return jax.shard_map(
        body,
        mesh=mesh,
        in_specs=(P("row", "col"), P(None, ("row", "col"), None), P()),
        out_specs=P("row", "col"),
        check_vma=False,
    )
```

```python
import jax
import jax.numpy as jnp
from jax import lax
from jax.experimental import pallas as pl
from jax.experimental.pallas import tpu as pltpu
from jax.sharding import PartitionSpec as P

MESH = pl.DeviceIdType.MESH
F32 = jnp.float32
BF16 = jnp.bfloat16
NN = ((1,), (0,))
TN = ((0,), (0,))


def split(value):
    high = value.astype(BF16)
    return high, (value - high.astype(F32)).astype(BF16)


def dot3(left, right, dims=NN):
    (lh, ll), (rh, rl) = left, right

    def one(a, b):
        return lax.dot_general(a, b, (dims, ((), ())), preferred_element_type=F32)

    return one(lh, rh) + (one(lh, rl) + one(ll, rh))


def dot_full(left, right):
    return jnp.dot(
        left, right, precision=lax.Precision.HIGHEST, preferred_element_type=F32
    )


def exchange_kernel(
    mat, vec, tf, a2, pi, zh_out, zl_out,
    a, vi, vj, pj, part, xb, total, hx, q, qr, yb, qz, zb,
    sp_, s1, s128, sx, s32, sy, s8, sz, sfull, tfv,
    send_sem, load_sem, zr, yr, cr, l2r, xr, rsr, hr, qcr, yqr, zqr,
    s1r, sxr, syr, szr, s4r, s5r, s6r,
):
    row, col = lax.axis_index("row"), lax.axis_index("col")
    x, zh = lax.div(row, 2), lax.rem(row, 2)
    y, zl, c = lax.div(col, 8), lax.rem(lax.div(col, 2), 4), lax.rem(col, 2)

    def mod4(v):
        return lax.rem(v + 8, 4)

    def dev(x_, zh_, y_, zl_, c_):
        return (x_ * 2 + zh_, (y_ * 4 + zl_) * 2 + c_)

    partner = dev(x, zh, y, zl, 1 - c)

    def at_x(k):
        return dev(mod4(x + k), zh, y, zl, c)

    def at_y(k):
        return dev(x, zh, mod4(y + k), zl, c)

    zk = [zl, zl + 1 - 2 * lax.rem(zl, 2), mod4(zl + 2), 3 - zl]
    yn = [y, mod4(y - 1), mod4(y + 1), mod4(y + 2)]

    def at_zl(k):
        return dev(x, zh, y, zk[k], c)

    def at_z(k):
        z = lax.rem(zh * 4 + zl + k, 8)
        return dev(x, lax.div(z, 4), y, lax.rem(z, 4), c)

    def spread_to(h):
        return dev(zl, h, x, 2 * zh + lax.div(y, 2), lax.rem(y, 2))

    def spread_from(h):
        return dev(y, lax.div(zl, 2), lax.rem(zl, 2) * 2 + c, x, h)

    def is_me(d):
        return jnp.logical_and(d[0] == row, d[1] == col)

    def rows(ref, start, count):
        return ref.at[pl.ds(pl.multiple_of(start, 8), count)]

    sent = []

    def send(src, dst, sem, device):
        copy = pltpu.make_async_remote_copy(
            src_ref=src, dst_ref=dst, send_sem=send_sem.at[len(sent)], recv_sem=sem,
            device_id=device, device_id_type=MESH,
        )
        copy.start()
        sent.append((copy, None))

    def send_or_keep(src, dst, sem, device):
        mine = is_me(device)
        copy = pltpu.make_async_remote_copy(
            src_ref=src, dst_ref=dst, send_sem=send_sem.at[len(sent)], recv_sem=sem,
            device_id=device, device_id_type=MESH,
        )
        keep = pltpu.make_async_copy(src, dst, sem)

        @pl.when(mine)
        def _():
            keep.start()

        @pl.when(jnp.logical_not(mine))
        def _():
            copy.start()

        sent.append((copy, jnp.logical_not(mine)))

    def finish():
        for copy, when in sent:
            if when is None:
                copy.wait_send()
            else:

                @pl.when(when)
                def _(copy=copy):
                    copy.wait_send()

    def arrived(dst, sem):
        pltpu.make_async_copy(dst, dst, sem).wait()

    load_a = pltpu.make_async_copy(mat, a, load_sem.at[0])
    load_t = pltpu.make_async_copy(tf, tfv, load_sem.at[3])
    load_v = [
        pltpu.make_async_copy(
            vec.at[p],
            vi.at[pl.ds(pl.multiple_of(col * 64, 8), 64), pl.ds(128 * p, 128)],
            load_sem.at[1 + p],
        )
        for p in range(2)
    ]
    for copy in load_v:
        copy.start()
    load_a.start()
    load_t.start()

    barrier = pltpu.get_barrier_semaphore()
    peers = [partner] + [at_x(k) for k in (1, 2, 3)] + [at_y(k) for k in (1, 2, 3)]
    peers += [at_z(k) for k in range(1, 8)]
    for peer in peers:
        pl.semaphore_signal(barrier, inc=1, device_id=peer, device_id_type=MESH)
    others = [f(h) for f in (spread_to, spread_from) for h in range(2)]
    for peer in others:

        @pl.when(jnp.logical_not(is_me(peer)))
        def _(peer=peer):
            pl.semaphore_signal(barrier, inc=1, device_id=peer, device_id_type=MESH)

    for copy in load_v:
        copy.wait()
    count = len(peers) + len(others)
    for peer in others:
        count = count - is_me(peer).astype(jnp.int32)
    pl.semaphore_wait(barrier, count)

    class Gather:
        def __init__(self, n, big, place):
            self.n, self.big, self.place = n, big, place

        def blk(self, y_, zl_, c_):
            return rows(self.big, self.place(y_, zl_, c_) * 64, 64)

        def half(self, y_, zl_, c_, h):
            return rows(self.big, self.place(y_, zl_, c_) * 64 + 32 * h, 32)

        def to_partner(self, n, k):
            b = self.blk(yn[n], zk[k], c)
            send(b, b, cr.at[self.n, n, k], partner)

        def to_y(self, k):
            b = self.blk(y, zk[k], c)
            send(b, b, yr.at[self.n, k, 0], at_y(1))
            send(b, b, yr.at[self.n, k, 1], at_y(3))

        def start(self):
            b = self.blk(y, zl, c)
            for k in (1, 2, 3):
                send(b, b, zr.at[self.n, k - 1], at_zl(k))
            self.to_y(0)
            self.to_partner(0, 0)

        def z_step(self, k):
            arrived(self.blk(y, zk[k], c), zr.at[self.n, k - 1])
            self.to_y(k)
            self.to_partner(0, k)

        def y_step(self, k):
            arrived(self.blk(yn[1], zk[k], c), yr.at[self.n, k, 0])
            h = self.half(yn[1], zk[k], c, 0)
            send(h, h, yr.at[self.n, k, 2], at_y(1))
            self.to_partner(1, k)
            arrived(self.blk(yn[2], zk[k], c), yr.at[self.n, k, 1])
            h = self.half(yn[2], zk[k], c, 1)
            send(h, h, yr.at[self.n, k, 3], at_y(3))
            self.to_partner(2, k)

        def y_last(self, k):
            for h in range(2):
                arrived(self.half(yn[3], zk[k], c, h), yr.at[self.n, k, 2 + h])
            self.to_partner(3, k)

        def from_partner(self, n):
            for k in range(4):
                arrived(self.blk(yn[n], zk[k], 1 - c), cr.at[self.n, n, k])

    class Ring:
        def __init__(self, n, small):
            self.n, self.small = n, small

        def start(self):
            b = rows(self.small, x * 128, 128)
            send(b, b, xr.at[self.n, 0], at_x(1))
            send(b, b, xr.at[self.n, 1], at_x(3))

        def step(self):
            m = mod4(x - 1)
            arrived(rows(self.small, m * 128, 128), xr.at[self.n, 0])
            h = rows(self.small, m * 128, 64)
            send(h, h, xr.at[self.n, 2], at_x(1))
            m = mod4(x + 1)
            arrived(rows(self.small, m * 128, 128), xr.at[self.n, 1])
            h = rows(self.small, m * 128 + 64, 64)
            send(h, h, xr.at[self.n, 3], at_x(3))

        def last(self):
            m = mod4(x + 2)
            for h in range(2):
                arrived(rows(self.small, m * 128 + 64 * h, 64), xr.at[self.n, 2 + h])

    class Sum:
        def __init__(self, at, piece, buf, sem):
            self.at, self.piece, self.buf, self.sem = at, piece, buf, sem

        def first(self):
            send(self.piece(2, 0), self.buf(0), self.sem(0), self.at(1))
            send(self.piece(2, 1), self.buf(1), self.sem(1), self.at(3))
            send(self.piece(1, 1), self.buf(2), self.sem(2), self.at(1))
            send(self.piece(3, 0), self.buf(3), self.sem(3), self.at(3))

        def second(self):
            for h, k, to in ((0, 1, 1), (1, 3, 3)):
                arrived(self.buf(h), self.sem(h))
                self.buf(6 + h)[...] = self.buf(h)[...] + self.piece(k, h)[...]
                send(self.buf(6 + h), self.buf(4 + h), self.sem(4 + h), self.at(to))

        def last(self, out):
            for h in range(2):
                arrived(self.buf(3 - h), self.sem(3 - h))
                arrived(self.buf(4 + h), self.sem(4 + h))
                out(h)[...] = self.piece(0, h)[...] + (self.buf(4 + h)[...] + self.buf(3 - h)[...])

    def place(y_, zl_, c_):
        return (y_ * 4 + zl_) * 2 + c_

    gv = Gather(0, vi, place)
    rv = Ring(0, vj)
    for h in range(2):
        send_or_keep(
            gv.blk(y, zl, c), rows(vj, (2 * zl + c) * 64, 64), l2r.at[c], spread_to(h)
        )
    gv.start()
    for k in (1, 2, 3):
        gv.z_step(k)
    for h in range(2):
        arrived(rows(vj, (2 * x + h) * 64, 64), l2r.at[h])
    rv.start()
    for k in range(4):
        gv.y_step(k)
    rv.step()
    for k in range(4):
        gv.y_last(k)
    load_a.wait()
    load_t.wait()
    rv.last()

    v_s = split(vj[...])
    gq = Gather(2, q, place)
    gr = Gather(2, qr, place)
    for n in (3, 1, 2, 0):
        span = pl.ds(pl.multiple_of(yn[n] * 512, 512), 512)
        q[span, :] = dot3(split(a[span, :]), v_s)
        for k in (3, 2, 1, 0):
            send(
                gq.blk(yn[n], zk[k], 1 - c), gr.blk(yn[n], zk[k], 1 - c), qcr.at[n, k], partner
            )
    ysum = []
    for k in (3, 2, 1, 0):
        for n in (3, 1, 2, 0):
            arrived(gr.blk(yn[n], zk[k], c), qcr.at[n, k])
            b = gq.blk(yn[n], zk[k], c)
            b[...] = b[...] + gr.blk(yn[n], zk[k], c)[...]
        ysum.append(
            Sum(
                at_y,
                lambda m, h, k=k: gq.half(mod4(y + m), zk[k], c, h),
                lambda m, k=k: yb.at[k, m],
                lambda m, k=k: yqr.at[k, m],
            )
        )
        ysum[-1].first()

    def chunk(n):
        start = pl.multiple_of(yn[n] * 512, 512)
        vt = vi[pl.ds(start, 512), :].T
        return dot3(split(vt), split(a[pl.ds(start, 512), :]))

    gv.from_partner(0)
    pt = chunk(0)
    gv.from_partner(1)
    pt += chunk(1)
    gv.from_partner(2)
    pt += chunk(2)
    gv.from_partner(3)
    pt += chunk(3)
    part[...] = pt.T
    xsum = Sum(
        at_x,
        lambda m, h: rows(part, mod4(x + m) * 128 + 64 * h, 64),
        lambda m: xb.at[m],
        lambda m: rsr.at[m],
    )
    xsum.first()
    ysum[0].second()
    ysum[1].second()

    sp_[...] = dot3(split(vj[...].T), split(part[...]))
    own = gv.blk(y, zl, c)[...]
    sp_[128:256, 0:128] = dot3(split(own[:, :128].T), split(own[:, 128:]))
    send(rows(sp_, 128 * (1 - c), 128), s1, s1r, partner)
    ysum[2].second()
    ysum[3].second()
    arrived(s1, s1r)
    s128[...] = rows(sp_, 128 * c, 128)[...] + s1[...]
    for k in (1, 2, 3):
        send(rows(s128, 32 * mod4(x + k), 32), sx.at[k - 1], sxr.at[k - 1], at_x(k))
    xsum.second()

    for m, k in enumerate((3, 2, 1, 0)):
        ysum[m].last(lambda h, k=k: qz.at[k, pl.ds(32 * h, 32)])
        if k:
            send(qz.at[k], zb.at[k - 1], zqr.at[k - 1], at_zl(k))
    for k in range(3):
        arrived(sx.at[k], sxr.at[k])
    s32[...] = rows(s128, 32 * x, 32)[...] + sx[0] + (sx[1] + sx[2])
    for k in (1, 2, 3):
        send(rows(s32, 8 * mod4(y + k), 8), sy.at[k - 1], syr.at[k - 1], at_y(k))
    xsum.last(lambda h: total.at[pl.ds(64 * h, 64)])
    send(total, hx, hr, at_z(4))
    for k in range(3):
        arrived(zb.at[k], zqr.at[k])
    gp = Gather(1, pi, place)
    gp.blk(y, zl, c)[...] = (qz[0] + zb[0]) + (zb[1] + zb[2])
    gp.start()

    for k in range(3):
        arrived(sy.at[k], syr.at[k])
    s8[...] = rows(s32, 8 * y, 8)[...] + sy[0] + (sy[1] + sy[2])
    for k in range(1, 8):
        send(s8, sz.at[k - 1], szr.at[k - 1], at_z(k))
    arrived(hx, hr)
    rp = Ring(1, pj)
    rows(pj, x * 128, 128)[...] = total[...] + hx[...]
    rp.start()

    def srow(x_, y_, c_):
        return rows(sfull, 128 * c_ + 32 * x_ + 8 * y_, 8)

    gp.z_step(1)
    for k in range(7):
        arrived(sz.at[k], szr.at[k])
    srow(x, y, c)[...] = s8[...] + sz[0] + (sz[1] + sz[2]) + ((sz[3] + sz[4]) + (sz[5] + sz[6]))
    for k in (1, 2, 3):
        send(srow(x, y, c), srow(x, y, c), s4r.at[k - 1], at_y(k))
    gp.z_step(2)
    gp.z_step(3)
    rp.step()
    for k in (1, 2, 3):
        arrived(srow(x, mod4(y - k), c), s4r.at[k - 1])
    s_own = rows(sfull, 128 * c + 32 * x, 32)
    for k in (1, 2, 3):
        send(s_own, s_own, s5r.at[k - 1], at_x(k))
    send(s_own, s_own, s6r.at[0], partner)
    gp.y_step(0)
    for k in (1, 2, 3):
        s_k = rows(sfull, 128 * c + 32 * mod4(x - k), 32)
        arrived(s_k, s5r.at[k - 1])
        send(s_k, s_k, s6r.at[k], partner)
    rp.last()
    gp.y_step(1)
    for k in range(4):
        arrived(rows(sfull, 128 * (1 - c) + 32 * mod4(x - k), 32), s6r.at[k])

    upper = lax.broadcasted_iota(jnp.int32, (128, 128), 0) <= lax.broadcasted_iota(
        jnp.int32, (128, 128), 1
    )
    t1 = jnp.where(upper, tfv[0], 0.0)
    t2 = jnp.where(upper, tfv[1], 0.0)
    s11, s12 = sfull[0:128, 0:128], sfull[0:128, 128:256]
    n12, s22 = sfull[128:256, 0:128], sfull[128:256, 128:256]
    t1t, t2t = t1.T, t2.T
    b = dot_full(t1t, dot_full(s11, t1))
    e = dot_full(t1t, s12)
    h = dot_full(b.T, n12)
    gp.y_step(2)
    nt2 = dot_full(n12, t2)
    f = dot_full(n12.T, e - 0.5 * h)
    k12 = dot_full(h - e, t2)
    m12 = -dot_full(t1, nt2)
    b2 = dot_full(t2t, dot_full(s22 - f - f.T, t2))
    gp.y_step(3)
    zero = jnp.zeros((128, 128), F32)
    kk = jnp.concatenate(
        [
            jnp.concatenate([-0.5 * (b + b.T), k12], axis=1),
            jnp.concatenate([k12.T, -0.5 * (b2 + b2.T)], axis=1),
        ],
        axis=0,
    )
    mm = jnp.concatenate(
        [jnp.concatenate([t1, m12], axis=1), jnp.concatenate([zero, t2], axis=1)], axis=0
    )
    xj = dot3(split(pj[...]), split(mm)) + dot3(v_s, split(kk))
    zj = dot3(v_s, split(mm.T))
    zh_out[...], zl_out[...] = split(zj.T)
    x_s = split(xj.T)
    gp.y_last(0)
    gp.y_last(1)
    for n in range(4):
        r = slice(512 * n, 512 * n + 512)
        a2[r, :] = a[r, :] - dot3(split(vi[r, :]), x_s)
        if n == 0:
            gp.y_last(2)
            gp.y_last(3)
    for n in range(4):
        gp.from_partner(n)
    finish()


def exchange(matrix, vectors, tfactor):
    def vmem(*shape):
        return pltpu.VMEM(shape, F32)

    def dma(*shape):
        return pltpu.SemaphoreType.DMA(shape)

    return pl.pallas_call(
        exchange_kernel,
        out_shape=(
            jax.ShapeDtypeStruct((2048, 512), F32),
            jax.ShapeDtypeStruct((2048, 256), F32),
            jax.ShapeDtypeStruct((256, 512), BF16),
            jax.ShapeDtypeStruct((256, 512), BF16),
        ),
        in_specs=[pl.BlockSpec(memory_space=pltpu.HBM)] * 3,
        out_specs=(pl.BlockSpec(memory_space=pltpu.VMEM),) * 4,
        scratch_shapes=[
            vmem(2048, 512), vmem(2048, 256), vmem(512, 256), vmem(512, 256), vmem(512, 256),
            vmem(8, 64, 256), vmem(128, 256), vmem(128, 256),
            vmem(2048, 256), vmem(2048, 256), vmem(4, 8, 32, 256), vmem(4, 64, 256), vmem(3, 64, 256),
            vmem(256, 256), vmem(128, 256), vmem(128, 256), vmem(3, 32, 256), vmem(32, 256),
            vmem(3, 8, 256), vmem(8, 256), vmem(7, 8, 256), vmem(256, 256), vmem(2, 128, 128),
            dma(190), dma(4), dma(2, 3), dma(2, 4, 4), dma(2, 4, 4), dma(2), dma(2, 4),
            dma(6), dma(), dma(4, 4), dma(4, 6), dma(3),
            dma(), dma(3), dma(3), dma(7), dma(3), dma(3), dma(4),
        ],
        compiler_params=pltpu.CompilerParams(
            collective_id=0, has_side_effects=True, vmem_limit_bytes=36 << 20
        ),
    )(*(pltpu.with_memory_space_constraint(v, pltpu.HBM) for v in (matrix, vectors, tfactor)))


def update_kernel(mat, pi, zh, zl, out):
    out[...] = mat[...] - dot3(split(pi[...]), (zh[...], zl[...]))


def update(matrix, pi, zh, zl):
    rows_here, cols_here = matrix.shape
    step = 512
    return pl.pallas_call(
        update_kernel,
        grid=(rows_here // step,),
        out_shape=jax.ShapeDtypeStruct(matrix.shape, F32),
        in_specs=[
            pl.BlockSpec((step, cols_here), lambda i: (i, 0)),
            pl.BlockSpec((step, 256), lambda i: (i, 0)),
            pl.BlockSpec((256, 512), lambda i: (0, 0)),
            pl.BlockSpec((256, 512), lambda i: (0, 0)),
        ],
        out_specs=pl.BlockSpec((step, cols_here), lambda i: (i, 0)),
        compiler_params=pltpu.CompilerParams(vmem_limit_bytes=20 << 20),
    )(matrix, pi, zh, zl)


def body(matrix, vectors, tfactor):
    return update(*exchange(matrix, vectors, tfactor))


def solution(mesh):
    return jax.shard_map(
        body,
        mesh=mesh,
        in_specs=(P("row", "col"), P(None, ("row", "col"), None), P()),
        out_specs=P("row", "col"),
        check_vma=False,
    )
```

```python
import jax
import jax.numpy as jnp
from jax import lax
from jax.experimental import pallas as pl
from jax.experimental.pallas import tpu as pltpu
from jax.sharding import PartitionSpec as P

MESH = pl.DeviceIdType.MESH
F32 = jnp.float32
BF16 = jnp.bfloat16
NN = ((1,), (0,))
TN = ((0,), (0,))


def split(value):
    high = value.astype(BF16)
    return high, (value - high.astype(F32)).astype(BF16)


def dot3(left, right, dims=NN):
    (lh, ll), (rh, rl) = left, right

    def one(a, b):
        return lax.dot_general(a, b, (dims, ((), ())), preferred_element_type=F32)

    return one(lh, rh) + (one(lh, rl) + one(ll, rh))


def dot_full(left, right):
    return dot3(split(left), split(right))


def exchange_kernel(
    mat, vec, tf, a2, pi, zh_out, zl_out,
    a, vi, vj, pj, part, xb, total, hx,
    sp_, s1, s128, sx, s32, sy, s8, sz, sfull, tfv,
    send_sem, load_sem, zr, yr, cr, l2r, xr, rsr, l1r, hr, s1r, sxr, syr, szr, s4r, s5r, s6r,
):
    row, col = lax.axis_index("row"), lax.axis_index("col")
    x, zh = lax.div(row, 2), lax.rem(row, 2)
    y, zl, c = lax.div(col, 8), lax.rem(lax.div(col, 2), 4), lax.rem(col, 2)

    def mod4(v):
        return lax.rem(v + 8, 4)

    def dev(x_, zh_, y_, zl_, c_):
        return (x_ * 2 + zh_, (y_ * 4 + zl_) * 2 + c_)

    partner = dev(x, zh, y, zl, 1 - c)

    def at_x(k):
        return dev(mod4(x + k), zh, y, zl, c)

    def at_y(k):
        return dev(x, zh, mod4(y + k), zl, c)

    zk = [zl, zl + 1 - 2 * lax.rem(zl, 2), 2 - lax.div(zl, 2), 3 - 3 * lax.div(zl, 2)]
    middle = jnp.logical_and(zl > 0, zl < 3)
    yn = [y, mod4(y - 1), mod4(y + 1), mod4(y + 2)]

    def at_zl(k):
        return dev(x, zh, y, zk[k], c)

    def at_z(k):
        z = lax.rem(zh * 4 + zl + k, 8)
        return dev(x, lax.div(z, 4), y, lax.rem(z, 4), c)

    def spread_to(h):
        return dev(zl, h, x, 2 * zh + lax.div(y, 2), lax.rem(y, 2))

    def spread_from(h):
        return dev(y, lax.div(zl, 2), lax.rem(zl, 2) * 2 + c, x, h)

    owner = dev(y, lax.div(zl, 2), x, 2 * zh + lax.rem(zl, 2), c)
    owned_from = dev(y, lax.div(zl, 2), x, 2 * zh + lax.rem(zl, 2), c)

    def is_me(d):
        return jnp.logical_and(d[0] == row, d[1] == col)

    def rows(ref, start, count):
        return ref.at[pl.ds(pl.multiple_of(start, 8), count)]

    sent = []

    def send(src, dst, sem, device, when=None):
        copy = pltpu.make_async_remote_copy(
            src_ref=src, dst_ref=dst, send_sem=send_sem.at[len(sent)], recv_sem=sem,
            device_id=device, device_id_type=MESH,
        )
        if when is None:
            copy.start()
        else:

            @pl.when(when)
            def _():
                copy.start()

        sent.append((copy, when))

    def send_or_keep(src, dst, sem, device):
        mine = is_me(device)
        copy = pltpu.make_async_remote_copy(
            src_ref=src, dst_ref=dst, send_sem=send_sem.at[len(sent)], recv_sem=sem,
            device_id=device, device_id_type=MESH,
        )
        keep = pltpu.make_async_copy(src, dst, sem)

        @pl.when(mine)
        def _():
            keep.start()

        @pl.when(jnp.logical_not(mine))
        def _():
            copy.start()

        sent.append((copy, jnp.logical_not(mine)))

    def finish():
        for copy, when in sent:
            if when is None:
                copy.wait_send()
            else:

                @pl.when(when)
                def _(copy=copy):
                    copy.wait_send()

    def arrived(dst, sem):
        pltpu.make_async_copy(dst, dst, sem).wait()

    load_a = pltpu.make_async_copy(mat, a, load_sem.at[0])
    load_t = pltpu.make_async_copy(tf, tfv, load_sem.at[3])
    load_v = [
        pltpu.make_async_copy(
            vec.at[p],
            vi.at[pl.ds(pl.multiple_of(col * 64, 8), 64), pl.ds(128 * p, 128)],
            load_sem.at[1 + p],
        )
        for p in range(2)
    ]
    for copy in load_v:
        copy.start()
    load_a.start()
    load_t.start()

    barrier = pltpu.get_barrier_semaphore()
    peers = [partner] + [at_x(k) for k in (1, 2, 3)] + [at_y(k) for k in (1, 2, 3)]
    peers += [at_z(k) for k in range(1, 8)]
    for peer in peers:
        pl.semaphore_signal(barrier, inc=1, device_id=peer, device_id_type=MESH)
    others = [f(h) for f in (spread_to, spread_from) for h in range(2)] + [owner, owned_from]
    for peer in others:

        @pl.when(jnp.logical_not(is_me(peer)))
        def _(peer=peer):
            pl.semaphore_signal(barrier, inc=1, device_id=peer, device_id_type=MESH)

    for copy in load_v:
        copy.wait()
    count = len(peers) + len(others)
    for peer in others:
        count = count - is_me(peer).astype(jnp.int32)
    pl.semaphore_wait(barrier, count)

    class Gather:
        def __init__(self, n, big, place):
            self.n, self.big, self.place = n, big, place

        def blk(self, y_, zl_, c_):
            return rows(self.big, self.place(y_, zl_, c_) * 64, 64)

        def half(self, y_, zl_, c_, h):
            return rows(self.big, self.place(y_, zl_, c_) * 64 + 32 * h, 32)

        def to_partner(self, n, k):
            b = self.blk(yn[n], zk[k], c)
            send(b, b, cr.at[self.n, n, k], partner)

        def to_y(self, k):
            for h, s in ((0, 0), (1, 1)):
                b = self.half(y, zk[k], c, h)
                send(b, b, yr.at[self.n, k, s], at_y(1))
            for h, s in ((1, 2), (0, 3)):
                b = self.half(y, zk[k], c, h)
                send(b, b, yr.at[self.n, k, s], at_y(3))

        def to_z(self, k, n, h, when):
            b = self.half(y, zk[k], c, h)
            sem = {(0, 1): 0, (0, 2): 1, (1, 2): 2, (2, 1): 1, (3, 1): 2}[k, n]
            send(b, b, zr.at[self.n, sem, h], at_zl(n), when)

        def start(self):
            for h in range(2):
                self.to_z(0, 1, h, None)
                self.to_z(0, 2, h, middle)
            self.to_y(0)
            self.to_partner(0, 0)

        def z_step(self, k):
            for h in range(2):
                arrived(self.half(y, zk[k], c, h), zr.at[self.n, k - 1, h])
                self.to_z(k, 2 if k == 1 else 1, h, middle)
            self.to_y(k)
            self.to_partner(0, k)

        def y_step(self, k):
            for n, h, s, to in ((1, 0, 0, 1), (2, 1, 2, 3)):
                b = self.half(yn[n], zk[k], c, h)
                arrived(b, yr.at[self.n, k, s])
                send(b, b, yr.at[self.n, k, 4 + h], at_y(to))
            for n, h, s in ((1, 1, 1), (2, 0, 3)):
                arrived(self.half(yn[n], zk[k], c, h), yr.at[self.n, k, s])
                self.to_partner(n, k)

        def y_last(self, k):
            for h in range(2):
                arrived(self.half(yn[3], zk[k], c, h), yr.at[self.n, k, 4 + h])
            self.to_partner(3, k)

        def from_partner(self, n):
            for k in range(4):
                arrived(self.blk(yn[n], zk[k], 1 - c), cr.at[self.n, n, k])

    class Ring:
        def __init__(self, n, small):
            self.n, self.small = n, small

        def half(self, k, h):
            return rows(self.small, mod4(x + k) * 128 + 64 * h, 64)

        def start(self):
            for h, s, to in ((0, 0, 1), (1, 2, 3), (1, 1, 1), (0, 3, 3)):
                b = self.half(0, h)
                send(b, b, xr.at[self.n, s], at_x(to))

        def step(self):
            for k, h, s, to in ((-1, 0, 0, 1), (1, 1, 2, 3)):
                b = self.half(k, h)
                arrived(b, xr.at[self.n, s])
                send(b, b, xr.at[self.n, 4 + h], at_x(to))

        def last(self):
            for k, h, s in ((-1, 1, 1), (1, 0, 3), (2, 0, 4), (2, 1, 5)):
                arrived(self.half(k, h), xr.at[self.n, s])

    class Sum:
        def __init__(self, at, piece, buf, sem):
            self.at, self.piece, self.buf, self.sem = at, piece, buf, sem

        def first(self):
            send(self.piece(2, 0), self.buf(0), self.sem(0), self.at(1))
            send(self.piece(2, 1), self.buf(1), self.sem(1), self.at(3))
            send(self.piece(1, 1), self.buf(2), self.sem(2), self.at(1))
            send(self.piece(3, 0), self.buf(3), self.sem(3), self.at(3))

        def second(self):
            for h, k, to in ((0, 1, 1), (1, 3, 3)):
                arrived(self.buf(h), self.sem(h))
                self.buf(6 + h)[...] = self.buf(h)[...] + self.piece(k, h)[...]
                send(self.buf(6 + h), self.buf(4 + h), self.sem(4 + h), self.at(to))

        def last(self, out):
            for h in range(2):
                arrived(self.buf(3 - h), self.sem(3 - h))
                arrived(self.buf(4 + h), self.sem(4 + h))
                out(h)[...] = self.piece(0, h)[...] + (self.buf(4 + h)[...] + self.buf(3 - h)[...])

    gv = Gather(0, vi, lambda y_, zl_, c_: (y_ * 4 + zl_) * 2 + c_)
    rv = Ring(0, vj)
    gv.start()
    for h in range(2):
        send_or_keep(
            gv.blk(y, zl, c), rows(vj, (2 * zl + c) * 64, 64), l2r.at[c], spread_to(h)
        )
    for k in (1, 2, 3):
        gv.z_step(k)
    for k in range(3):
        gv.y_step(k)
    for h in range(2):
        arrived(rows(vj, (2 * x + h) * 64, 64), l2r.at[h])
    rv.start()
    gv.y_step(3)
    load_a.wait()
    load_t.wait()

    def chunk(n):
        start = pl.multiple_of(yn[n] * 512, 512)
        vt = vi[pl.ds(start, 512), :].T
        return dot3(split(vt), split(a[pl.ds(start, 512), :]))

    gv.from_partner(0)
    pt = chunk(0)
    rv.step()
    for k in range(4):
        gv.y_last(k)
    gv.from_partner(1)
    pt += chunk(1)
    gv.from_partner(2)
    pt += chunk(2)
    gv.from_partner(3)
    pt += chunk(3)
    part[...] = pt.T

    xsum = Sum(
        at_x,
        lambda m, h: rows(part, mod4(x + m) * 128 + 64 * h, 64),
        lambda m: xb.at[m],
        lambda m: rsr.at[m],
    )
    xsum.first()

    rv.last()
    sp_[...] = dot3(split(vj[...].T), split(part[...]))
    own = gv.blk(y, zl, c)[...]
    sp_[128:256, 0:128] = dot3(split(own[:, :128].T), split(own[:, 128:]))
    send(rows(sp_, 128 * (1 - c), 128), s1, s1r, partner)
    xsum.second()
    arrived(s1, s1r)
    s128[...] = rows(sp_, 128 * c, 128)[...] + s1[...]
    for k in (1, 2, 3):
        send(rows(s128, 32 * mod4(x + k), 32), sx.at[k - 1], sxr.at[k - 1], at_x(k))

    xsum.last(lambda h: total.at[pl.ds(64 * h, 64)])
    send(rows(total, 64 * (1 - zh), 64), hx, hr.at[0], at_z(4))
    for k in range(3):
        arrived(sx.at[k], sxr.at[k])
    s32[...] = rows(s128, 32 * x, 32)[...] + sx[0] + (sx[1] + sx[2])
    for k in (1, 2, 3):
        send(rows(s32, 8 * mod4(y + k), 8), sy.at[k - 1], syr.at[k - 1], at_y(k))
    for k in range(3):
        arrived(sy.at[k], syr.at[k])
    s8[...] = rows(s32, 8 * y, 8)[...] + sy[0] + (sy[1] + sy[2])
    for k in range(1, 8):
        send(s8, sz.at[k - 1], szr.at[k - 1], at_z(k))
    arrived(hx, hr.at[0])
    p_own = rows(pj, x * 128 + 64 * zh, 64)
    p_own[...] = rows(total, 64 * zh, 64)[...] + hx[...]
    gp = Gather(
        1, pi, lambda y_, zl_, c_: (lax.rem(zl_, 2) * 2 + c_) * 8 + 2 * y_ + lax.div(zl_, 2)
    )
    send_or_keep(p_own, gp.blk(x, 2 * zh + lax.rem(zl, 2), c), l1r, owner)
    send(p_own, p_own, hr.at[1], at_z(4))

    def srow(x_, y_, c_):
        return rows(sfull, 128 * c_ + 32 * x_ + 8 * y_, 8)

    for k in range(7):
        arrived(sz.at[k], szr.at[k])
    srow(x, y, c)[...] = s8[...] + sz[0] + (sz[1] + sz[2]) + ((sz[3] + sz[4]) + (sz[5] + sz[6]))
    for k in (1, 2, 3):
        send(srow(x, y, c), srow(x, y, c), s4r.at[k - 1], at_y(k))
    arrived(gp.blk(y, zl, c), l1r)
    gp.start()
    for k in (1, 2, 3):
        arrived(srow(x, mod4(y - k), c), s4r.at[k - 1])
    s_own = rows(sfull, 128 * c + 32 * x, 32)
    for k in (1, 2, 3):
        send(s_own, s_own, s5r.at[k - 1], at_x(k))
    send(s_own, s_own, s6r.at[0], partner)
    rp = Ring(1, pj)
    arrived(rows(pj, x * 128 + 64 * (1 - zh), 64), hr.at[1])
    rp.start()
    gp.z_step(1)
    for k in (1, 2, 3):
        s_k = rows(sfull, 128 * c + 32 * mod4(x - k), 32)
        arrived(s_k, s5r.at[k - 1])
        send(s_k, s_k, s6r.at[k], partner)
    gp.z_step(2)
    gp.z_step(3)
    for k in range(4):
        arrived(rows(sfull, 128 * (1 - c) + 32 * mod4(x - k), 32), s6r.at[k])

    upper = lax.broadcasted_iota(jnp.int32, (128, 128), 0) <= lax.broadcasted_iota(
        jnp.int32, (128, 128), 1
    )
    t1 = jnp.where(upper, tfv[0], 0.0)
    t2 = jnp.where(upper, tfv[1], 0.0)
    s11, s12 = sfull[0:128, 0:128], sfull[0:128, 128:256]
    n12, s22 = sfull[128:256, 0:128], sfull[128:256, 128:256]
    t1t, t2t = t1.T, t2.T
    b = dot_full(t1t, dot_full(s11, t1))
    e = dot_full(t1t, s12)
    nt2 = dot_full(n12, t2)
    gp.y_step(0)
    rp.step()
    h = dot_full(b.T, n12)
    k12 = dot_full(h - e, t2)
    m12 = -dot_full(t1, nt2)
    f = dot_full(n12.T, e - 0.5 * h)
    gp.y_step(1)
    b2 = dot_full(t2t, dot_full(s22 - f - f.T, t2))
    gp.y_step(2)
    zero = jnp.zeros((128, 128), F32)
    kk = jnp.concatenate(
        [
            jnp.concatenate([-0.5 * (b + b.T), k12], axis=1),
            jnp.concatenate([k12.T, -0.5 * (b2 + b2.T)], axis=1),
        ],
        axis=0,
    )
    mm = jnp.concatenate(
        [jnp.concatenate([t1, m12], axis=1), jnp.concatenate([zero, t2], axis=1)], axis=0
    )
    rp.last()
    v_s = split(vj[...])
    xj = dot3(split(pj[...]), split(mm)) + dot3(v_s, split(kk))
    x_s = split(xj.T)
    gp.y_step(3)
    zj = dot3(v_s, split(mm.T))
    zh_out[...], zl_out[...] = split(zj.T)
    for n in range(4):
        if n == 2:
            for k in range(4):
                gp.y_last(k)
        r = slice(512 * n, 512 * n + 512)
        a2[r, :] = a[r, :] - dot3(split(vi[r, :]), x_s)
    for n in range(4):
        gp.from_partner(n)
    finish()


def exchange(matrix, vectors, tfactor):
    def vmem(*shape):
        return pltpu.VMEM(shape, F32)

    def dma(*shape):
        return pltpu.SemaphoreType.DMA(shape)

    return pl.pallas_call(
        exchange_kernel,
        out_shape=(
            jax.ShapeDtypeStruct((2048, 512), F32),
            jax.ShapeDtypeStruct((2048, 256), F32),
            jax.ShapeDtypeStruct((256, 512), BF16),
            jax.ShapeDtypeStruct((256, 512), BF16),
        ),
        in_specs=[pl.BlockSpec(memory_space=pltpu.HBM)] * 3,
        out_specs=(pl.BlockSpec(memory_space=pltpu.VMEM),) * 4,
        scratch_shapes=[
            vmem(2048, 512), vmem(2048, 256), vmem(512, 256), vmem(512, 256), vmem(512, 256),
            vmem(8, 64, 256), vmem(128, 256), vmem(64, 256),
            vmem(256, 256), vmem(128, 256), vmem(128, 256), vmem(3, 32, 256), vmem(32, 256),
            vmem(3, 8, 256), vmem(8, 256), vmem(7, 8, 256), vmem(256, 256), vmem(2, 128, 128),
            dma(160), dma(4), dma(2, 3, 2), dma(2, 4, 6), dma(2, 4, 4), dma(2), dma(2, 6),
            dma(6), dma(), dma(2), dma(), dma(3), dma(3), dma(7), dma(3), dma(3), dma(4),
        ],
        compiler_params=pltpu.CompilerParams(
            collective_id=0, has_side_effects=True, vmem_limit_bytes=36 << 20
        ),
    )(*(pltpu.with_memory_space_constraint(v, pltpu.HBM) for v in (matrix, vectors, tfactor)))


def update_kernel(mat, pi, zh, zl, out):
    out[...] = mat[...] - dot3(split(pi[...]), (zh[...], zl[...]))


def update(matrix, pi, zh, zl):
    rows_here, cols_here = matrix.shape
    step = 512
    return pl.pallas_call(
        update_kernel,
        grid=(rows_here // step,),
        out_shape=jax.ShapeDtypeStruct(matrix.shape, F32),
        in_specs=[
            pl.BlockSpec((step, cols_here), lambda i: (i, 0)),
            pl.BlockSpec((step, 256), lambda i: (i, 0)),
            pl.BlockSpec((256, 512), lambda i: (0, 0)),
            pl.BlockSpec((256, 512), lambda i: (0, 0)),
        ],
        out_specs=pl.BlockSpec((step, cols_here), lambda i: (i, 0)),
        compiler_params=pltpu.CompilerParams(vmem_limit_bytes=20 << 20),
    )(matrix, pi, zh, zl)


def body(matrix, vectors, tfactor):
    return update(*exchange(matrix, vectors, tfactor))


def solution(mesh):
    return jax.shard_map(
        body,
        mesh=mesh,
        in_specs=(P("row", "col"), P(None, ("row", "col"), None), P()),
        out_specs=P("row", "col"),
        check_vma=False,
    )
```

```python
import jax
import jax.numpy as jnp
from jax import lax
from jax.experimental import pallas as pl
from jax.experimental.pallas import tpu as pltpu
from jax.sharding import PartitionSpec as P

MESH = pl.DeviceIdType.MESH
F32 = jnp.float32
BF16 = jnp.bfloat16
NN = ((1,), (0,))
DIRECT = (3,)
TN = ((0,), (0,))


def split(value):
    high = value.astype(BF16)
    return high, (value - high.astype(F32)).astype(BF16)


def dot3(left, right, dims=NN):
    (lh, ll), (rh, rl) = left, right

    def one(a, b):
        return lax.dot_general(a, b, (dims, ((), ())), preferred_element_type=F32)

    return one(lh, rh) + (one(lh, rl) + one(ll, rh))


def dot_full(left, right):
    return dot3(split(left), split(right))


def exchange_kernel(
    mat, vec, tf, a2, pi, zh_out, zl_out,
    a, vi, vj, pj, part, xb, total, hx,
    sp_, s1, s128, sx, s32, sy, s8, sz, sfull, tfv,
    send_sem, load_sem, zr, yr, cr, l2r, xr, rsr, l1r, hr, s1r, sxr, syr, szr, s4r, s5r, s6r,
):
    row, col = lax.axis_index("row"), lax.axis_index("col")
    x, zh = lax.div(row, 2), lax.rem(row, 2)
    y, zl, c = lax.div(col, 8), lax.rem(lax.div(col, 2), 4), lax.rem(col, 2)

    def mod4(v):
        return lax.rem(v + 8, 4)

    def dev(x_, zh_, y_, zl_, c_):
        return (x_ * 2 + zh_, (y_ * 4 + zl_) * 2 + c_)

    partner = dev(x, zh, y, zl, 1 - c)

    def at_x(k):
        return dev(mod4(x + k), zh, y, zl, c)

    def at_y(k):
        return dev(x, zh, mod4(y + k), zl, c)

    zk = [zl, zl + 1 - 2 * lax.rem(zl, 2), 2 - lax.div(zl, 2), 3 - 3 * lax.div(zl, 2)]
    middle = jnp.logical_and(zl > 0, zl < 3)
    yn = [y, mod4(y - 1), mod4(y + 1), mod4(y + 2)]

    def at_zl(k):
        return dev(x, zh, y, zk[k], c)

    def at_z(k):
        z = lax.rem(zh * 4 + zl + k, 8)
        return dev(x, lax.div(z, 4), y, lax.rem(z, 4), c)

    def spread_to(h):
        return dev(zl, h, x, 2 * zh + lax.div(y, 2), lax.rem(y, 2))

    def spread_from(h):
        return dev(y, lax.div(zl, 2), lax.rem(zl, 2) * 2 + c, x, h)

    owner = dev(y, lax.div(zl, 2), x, 2 * zh + lax.rem(zl, 2), c)
    owned_from = dev(y, lax.div(zl, 2), x, 2 * zh + lax.rem(zl, 2), c)

    def is_me(d):
        return jnp.logical_and(d[0] == row, d[1] == col)

    def rows(ref, start, count):
        return ref.at[pl.ds(pl.multiple_of(start, 8), count)]

    sent = []

    def send(src, dst, sem, device, when=None):
        copy = pltpu.make_async_remote_copy(
            src_ref=src, dst_ref=dst, send_sem=send_sem.at[len(sent)], recv_sem=sem,
            device_id=device, device_id_type=MESH,
        )
        if when is None:
            copy.start()
        else:

            @pl.when(when)
            def _():
                copy.start()

        sent.append((copy, when))

    def send_or_keep(src, dst, sem, device):
        mine = is_me(device)
        copy = pltpu.make_async_remote_copy(
            src_ref=src, dst_ref=dst, send_sem=send_sem.at[len(sent)], recv_sem=sem,
            device_id=device, device_id_type=MESH,
        )
        keep = pltpu.make_async_copy(src, dst, sem)

        @pl.when(mine)
        def _():
            keep.start()

        @pl.when(jnp.logical_not(mine))
        def _():
            copy.start()

        sent.append((copy, jnp.logical_not(mine)))

    def finish():
        for copy, when in sent:
            if when is None:
                copy.wait_send()
            else:

                @pl.when(when)
                def _(copy=copy):
                    copy.wait_send()

    def arrived(dst, sem):
        pltpu.make_async_copy(dst, dst, sem).wait()

    load_a = pltpu.make_async_copy(mat, a, load_sem.at[0])
    load_t = pltpu.make_async_copy(tf, tfv, load_sem.at[3])
    load_v = [
        pltpu.make_async_copy(
            vec.at[p],
            vi.at[pl.ds(pl.multiple_of(col * 64, 8), 64), pl.ds(128 * p, 128)],
            load_sem.at[1 + p],
        )
        for p in range(2)
    ]
    for copy in load_v:
        copy.start()
    load_a.start()
    load_t.start()

    barrier = pltpu.get_barrier_semaphore()
    peers = [partner] + [at_x(k) for k in (1, 2, 3)] + [at_y(k) for k in (1, 2, 3)]
    peers += [at_z(k) for k in range(1, 8)]
    for peer in peers:
        pl.semaphore_signal(barrier, inc=1, device_id=peer, device_id_type=MESH)
    others = [f(h) for f in (spread_to, spread_from) for h in range(2)] + [owner, owned_from]
    for peer in others:

        @pl.when(jnp.logical_not(is_me(peer)))
        def _(peer=peer):
            pl.semaphore_signal(barrier, inc=1, device_id=peer, device_id_type=MESH)

    for copy in load_v:
        copy.wait()
    count = len(peers) + len(others)
    for peer in others:
        count = count - is_me(peer).astype(jnp.int32)
    pl.semaphore_wait(barrier, count)

    class Gather:
        def __init__(self, n, big, place):
            self.n, self.big, self.place = n, big, place

        def blk(self, y_, zl_, c_):
            return rows(self.big, self.place(y_, zl_, c_) * 64, 64)

        def half(self, y_, zl_, c_, h):
            return rows(self.big, self.place(y_, zl_, c_) * 64 + 32 * h, 32)

        def to_partner(self, n, k):
            b = self.blk(yn[n], zk[k], c)
            send(b, b, cr.at[self.n, n, k], partner)

        def to_y(self, k):
            if k in DIRECT:
                b = self.blk(y, zk[k], c)
                for s, n in ((0, 1), (2, 3), (4, 2)):
                    send(b, b, yr.at[self.n, k, s], at_y(n))
                return
            for h, s in ((0, 0), (1, 1)):
                b = self.half(y, zk[k], c, h)
                send(b, b, yr.at[self.n, k, s], at_y(1))
            for h, s in ((1, 2), (0, 3)):
                b = self.half(y, zk[k], c, h)
                send(b, b, yr.at[self.n, k, s], at_y(3))

        def to_z(self, k, n, h, when):
            b = self.half(y, zk[k], c, h)
            sem = {(0, 1): 0, (0, 2): 1, (1, 2): 2, (2, 1): 1, (3, 1): 2}[k, n]
            send(b, b, zr.at[self.n, sem, h], at_zl(n), when)

        def start(self):
            for h in range(2):
                self.to_z(0, 1, h, None)
                self.to_z(0, 2, h, middle)
            self.to_y(0)
            self.to_partner(0, 0)

        def z_step(self, k):
            for h in range(2):
                arrived(self.half(y, zk[k], c, h), zr.at[self.n, k - 1, h])
                self.to_z(k, 2 if k == 1 else 1, h, middle)
            self.to_y(k)
            self.to_partner(0, k)

        def y_step(self, k):
            if k in DIRECT:
                for n, s in ((1, 0), (2, 2)):
                    arrived(self.blk(yn[n], zk[k], c), yr.at[self.n, k, s])
                    self.to_partner(n, k)
                return
            for n, h, s, to in ((1, 0, 0, 1), (2, 1, 2, 3)):
                b = self.half(yn[n], zk[k], c, h)
                arrived(b, yr.at[self.n, k, s])
                send(b, b, yr.at[self.n, k, 4 + h], at_y(to))
            for n, h, s in ((1, 1, 1), (2, 0, 3)):
                arrived(self.half(yn[n], zk[k], c, h), yr.at[self.n, k, s])
                self.to_partner(n, k)

        def y_last(self, k):
            if k in DIRECT:
                arrived(self.blk(yn[3], zk[k], c), yr.at[self.n, k, 4])
                self.to_partner(3, k)
                return
            for h in range(2):
                arrived(self.half(yn[3], zk[k], c, h), yr.at[self.n, k, 4 + h])
            self.to_partner(3, k)

        def from_partner(self, n):
            for k in range(4):
                arrived(self.blk(yn[n], zk[k], 1 - c), cr.at[self.n, n, k])

    class Ring:
        def __init__(self, n, small):
            self.n, self.small = n, small

        def own(self, k):
            return rows(self.small, mod4(x + k) * 128, 128)

        def start(self):
            for k in (1, 3, 2):
                send(self.own(0), self.own(0), xr.at[self.n, k - 1], at_x(k))

        def last(self):
            for k in (1, 3, 2):
                arrived(self.own(-k), xr.at[self.n, k - 1])

    class Sum:
        def __init__(self, at, piece, buf, sem):
            self.at, self.piece, self.buf, self.sem = at, piece, buf, sem

        def first(self):
            send(self.piece(2, 0), self.buf(0), self.sem(0), self.at(1))
            send(self.piece(2, 1), self.buf(1), self.sem(1), self.at(3))
            send(self.piece(1, 1), self.buf(2), self.sem(2), self.at(1))
            send(self.piece(3, 0), self.buf(3), self.sem(3), self.at(3))

        def second(self):
            for h, k, to in ((0, 1, 1), (1, 3, 3)):
                arrived(self.buf(h), self.sem(h))
                self.buf(6 + h)[...] = self.buf(h)[...] + self.piece(k, h)[...]
                send(self.buf(6 + h), self.buf(4 + h), self.sem(4 + h), self.at(to))

        def last(self, out):
            for h in range(2):
                arrived(self.buf(3 - h), self.sem(3 - h))
                arrived(self.buf(4 + h), self.sem(4 + h))
                out(h)[...] = self.piece(0, h)[...] + (self.buf(4 + h)[...] + self.buf(3 - h)[...])

    gv = Gather(0, vi, lambda y_, zl_, c_: (y_ * 4 + zl_) * 2 + c_)
    rv = Ring(0, vj)
    gv.start()
    for h in range(2):
        send_or_keep(
            gv.blk(y, zl, c), rows(vj, (2 * zl + c) * 64, 64), l2r.at[c], spread_to(h)
        )
    for k in (1, 2, 3):
        gv.z_step(k)
    for k in range(3):
        gv.y_step(k)
    for h in range(2):
        arrived(rows(vj, (2 * x + h) * 64, 64), l2r.at[h])
    rv.start()
    gv.y_step(3)
    load_a.wait()
    load_t.wait()

    def chunk(n):
        start = pl.multiple_of(yn[n] * 512, 512)
        vt = vi[pl.ds(start, 512), :].T
        return dot3(split(vt), split(a[pl.ds(start, 512), :]))

    gv.from_partner(0)
    pt = chunk(0)
    for k in range(4):
        gv.y_last(k)
    gv.from_partner(1)
    pt += chunk(1)
    gv.from_partner(2)
    pt += chunk(2)
    gv.from_partner(3)
    pt += chunk(3)
    part[...] = pt.T

    xsum = Sum(
        at_x,
        lambda m, h: rows(part, mod4(x + m) * 128 + 64 * h, 64),
        lambda m: xb.at[m],
        lambda m: rsr.at[m],
    )
    xsum.first()

    rv.last()
    sp_[...] = dot3(split(vj[...].T), split(part[...]))
    own = gv.blk(y, zl, c)[...]
    sp_[128:256, 0:128] = dot3(split(own[:, :128].T), split(own[:, 128:]))
    send(rows(sp_, 128 * (1 - c), 128), s1, s1r, partner)
    xsum.second()
    arrived(s1, s1r)
    s128[...] = rows(sp_, 128 * c, 128)[...] + s1[...]
    for k in (1, 2, 3):
        send(rows(s128, 32 * mod4(x + k), 32), sx.at[k - 1], sxr.at[k - 1], at_x(k))

    xsum.last(lambda h: total.at[pl.ds(64 * h, 64)])
    send(rows(total, 64 * (1 - zh), 64), hx, hr.at[0], at_z(4))
    for k in range(3):
        arrived(sx.at[k], sxr.at[k])
    s32[...] = rows(s128, 32 * x, 32)[...] + sx[0] + (sx[1] + sx[2])
    for k in (1, 2, 3):
        send(rows(s32, 8 * mod4(y + k), 8), sy.at[k - 1], syr.at[k - 1], at_y(k))
    for k in range(3):
        arrived(sy.at[k], syr.at[k])
    s8[...] = rows(s32, 8 * y, 8)[...] + sy[0] + (sy[1] + sy[2])
    for k in range(1, 8):
        send(s8, sz.at[k - 1], szr.at[k - 1], at_z(k))
    arrived(hx, hr.at[0])
    p_own = rows(pj, x * 128 + 64 * zh, 64)
    p_own[...] = rows(total, 64 * zh, 64)[...] + hx[...]
    gp = Gather(
        1, pi, lambda y_, zl_, c_: (lax.rem(zl_, 2) * 2 + c_) * 8 + 2 * y_ + lax.div(zl_, 2)
    )
    send_or_keep(p_own, gp.blk(x, 2 * zh + lax.rem(zl, 2), c), l1r, owner)
    send(p_own, p_own, hr.at[1], at_z(4))

    def srow(x_, y_, c_):
        return rows(sfull, 128 * c_ + 32 * x_ + 8 * y_, 8)

    for k in range(7):
        arrived(sz.at[k], szr.at[k])
    srow(x, y, c)[...] = s8[...] + sz[0] + (sz[1] + sz[2]) + ((sz[3] + sz[4]) + (sz[5] + sz[6]))
    for k in (1, 2, 3):
        send(srow(x, y, c), srow(x, y, c), s4r.at[k - 1], at_y(k))
    arrived(gp.blk(y, zl, c), l1r)
    gp.start()
    for k in (1, 2, 3):
        arrived(srow(x, mod4(y - k), c), s4r.at[k - 1])
    s_own = rows(sfull, 128 * c + 32 * x, 32)
    for k in (1, 2, 3):
        send(s_own, s_own, s5r.at[k - 1], at_x(k))
    send(s_own, s_own, s6r.at[0], partner)
    rp = Ring(1, pj)
    arrived(rows(pj, x * 128 + 64 * (1 - zh), 64), hr.at[1])
    rp.start()
    gp.z_step(1)
    for k in (1, 2, 3):
        s_k = rows(sfull, 128 * c + 32 * mod4(x - k), 32)
        arrived(s_k, s5r.at[k - 1])
        send(s_k, s_k, s6r.at[k], partner)
    gp.z_step(2)
    gp.z_step(3)
    for k in range(4):
        arrived(rows(sfull, 128 * (1 - c) + 32 * mod4(x - k), 32), s6r.at[k])

    upper = lax.broadcasted_iota(jnp.int32, (128, 128), 0) <= lax.broadcasted_iota(
        jnp.int32, (128, 128), 1
    )
    t1 = jnp.where(upper, tfv[0], 0.0)
    t2 = jnp.where(upper, tfv[1], 0.0)
    s11, s12 = sfull[0:128, 0:128], sfull[0:128, 128:256]
    n12, s22 = sfull[128:256, 0:128], sfull[128:256, 128:256]
    t1t, t2t = t1.T, t2.T
    b = dot_full(t1t, dot_full(s11, t1))
    e = dot_full(t1t, s12)
    nt2 = dot_full(n12, t2)
    gp.y_step(0)
    h = dot_full(b.T, n12)
    k12 = dot_full(h - e, t2)
    m12 = -dot_full(t1, nt2)
    f = dot_full(n12.T, e - 0.5 * h)
    gp.y_step(1)
    b2 = dot_full(t2t, dot_full(s22 - f - f.T, t2))
    gp.y_step(2)
    zero = jnp.zeros((128, 128), F32)
    kk = jnp.concatenate(
        [
            jnp.concatenate([-0.5 * (b + b.T), k12], axis=1),
            jnp.concatenate([k12.T, -0.5 * (b2 + b2.T)], axis=1),
        ],
        axis=0,
    )
    mm = jnp.concatenate(
        [jnp.concatenate([t1, m12], axis=1), jnp.concatenate([zero, t2], axis=1)], axis=0
    )
    rp.last()
    v_s = split(vj[...])
    xj = dot3(split(pj[...]), split(mm)) + dot3(v_s, split(kk))
    x_s = split(xj.T)
    gp.y_step(3)
    zj = dot3(v_s, split(mm.T))
    zh_out[...], zl_out[...] = split(zj.T)
    for n in range(4):
        if n == 2:
            for k in range(4):
                gp.y_last(k)
        r = slice(512 * n, 512 * n + 512)
        a2[r, :] = a[r, :] - dot3(split(vi[r, :]), x_s)
    for n in range(4):
        gp.from_partner(n)
    finish()


def exchange(matrix, vectors, tfactor):
    def vmem(*shape):
        return pltpu.VMEM(shape, F32)

    def dma(*shape):
        return pltpu.SemaphoreType.DMA(shape)

    return pl.pallas_call(
        exchange_kernel,
        out_shape=(
            jax.ShapeDtypeStruct((2048, 512), F32),
            jax.ShapeDtypeStruct((2048, 256), F32),
            jax.ShapeDtypeStruct((256, 512), BF16),
            jax.ShapeDtypeStruct((256, 512), BF16),
        ),
        in_specs=[pl.BlockSpec(memory_space=pltpu.HBM)] * 3,
        out_specs=(pl.BlockSpec(memory_space=pltpu.VMEM),) * 4,
        scratch_shapes=[
            vmem(2048, 512), vmem(2048, 256), vmem(512, 256), vmem(512, 256), vmem(512, 256),
            vmem(8, 64, 256), vmem(128, 256), vmem(64, 256),
            vmem(256, 256), vmem(128, 256), vmem(128, 256), vmem(3, 32, 256), vmem(32, 256),
            vmem(3, 8, 256), vmem(8, 256), vmem(7, 8, 256), vmem(256, 256), vmem(2, 128, 128),
            dma(160), dma(4), dma(2, 3, 2), dma(2, 4, 6), dma(2, 4, 4), dma(2), dma(2, 6),
            dma(6), dma(), dma(2), dma(), dma(3), dma(3), dma(7), dma(3), dma(3), dma(4),
        ],
        compiler_params=pltpu.CompilerParams(
            collective_id=0, has_side_effects=True, vmem_limit_bytes=36 << 20
        ),
    )(*(pltpu.with_memory_space_constraint(v, pltpu.HBM) for v in (matrix, vectors, tfactor)))


def update_kernel(mat, pi, zh, zl, out):
    out[...] = mat[...] - dot3(split(pi[...]), (zh[...], zl[...]))


def update(matrix, pi, zh, zl):
    rows_here, cols_here = matrix.shape
    step = 1024
    return pl.pallas_call(
        update_kernel,
        grid=(rows_here // step,),
        out_shape=jax.ShapeDtypeStruct(matrix.shape, F32),
        in_specs=[
            pl.BlockSpec((step, cols_here), lambda i: (i, 0)),
            pl.BlockSpec((step, 256), lambda i: (i, 0)),
            pl.BlockSpec((256, 512), lambda i: (0, 0)),
            pl.BlockSpec((256, 512), lambda i: (0, 0)),
        ],
        out_specs=pl.BlockSpec((step, cols_here), lambda i: (i, 0)),
        compiler_params=pltpu.CompilerParams(vmem_limit_bytes=20 << 20),
    )(matrix, pi, zh, zl)


def body(matrix, vectors, tfactor):
    return update(*exchange(matrix, vectors, tfactor))


def solution(mesh):
    return jax.shard_map(
        body,
        mesh=mesh,
        in_specs=(P("row", "col"), P(None, ("row", "col"), None), P()),
        out_specs=P("row", "col"),
        check_vma=False,
    )
```

```python
import jax
import jax.numpy as jnp
from jax import lax
from jax.experimental import pallas as pl
from jax.experimental.pallas import tpu as pltpu
from jax.sharding import PartitionSpec as P

MESH = pl.DeviceIdType.MESH
F32 = jnp.float32
BF16 = jnp.bfloat16
NN = ((1,), (0,))
DIRECT = (3,)
TN = ((0,), (0,))


def split(value):
    high = value.astype(BF16)
    return high, (value - high.astype(F32)).astype(BF16)


def dot3(left, right, dims=NN):
    (lh, ll), (rh, rl) = left, right

    def one(a, b):
        return lax.dot_general(a, b, (dims, ((), ())), preferred_element_type=F32)

    return one(lh, rh) + (one(lh, rl) + one(ll, rh))


def dot_full(left, right):
    return dot3(split(left), split(right))


def exchange_kernel(
    mat, vec, tf, a2, pi, zh_out, zl_out,
    a, vi, vj, pj, part, xb, total, hx,
    sp_, s1, s128, sx, s32, sy, s8, sz, sfull, tfv,
    send_sem, load_sem, zr, yr, cr, l2r, xr, rsr, l1r, hr, s1r, sxr, syr, szr, s4r, s5r, s6r,
):
    row, col = lax.axis_index("row"), lax.axis_index("col")
    x, zh = lax.div(row, 2), lax.rem(row, 2)
    y, zl, c = lax.div(col, 8), lax.rem(lax.div(col, 2), 4), lax.rem(col, 2)

    def mod4(v):
        return lax.rem(v + 8, 4)

    def dev(x_, zh_, y_, zl_, c_):
        return (x_ * 2 + zh_, (y_ * 4 + zl_) * 2 + c_)

    partner = dev(x, zh, y, zl, 1 - c)

    def at_x(k):
        return dev(mod4(x + k), zh, y, zl, c)

    def at_y(k):
        return dev(x, zh, mod4(y + k), zl, c)

    zk = [zl, zl + 1 - 2 * lax.rem(zl, 2), 2 - lax.div(zl, 2), 3 - 3 * lax.div(zl, 2)]
    middle = jnp.logical_and(zl > 0, zl < 3)
    yn = [y, mod4(y - 1), mod4(y + 1), mod4(y + 2)]

    def at_zl(k):
        return dev(x, zh, y, zk[k], c)

    def at_z(k):
        z = lax.rem(zh * 4 + zl + k, 8)
        return dev(x, lax.div(z, 4), y, lax.rem(z, 4), c)

    def spread_to(h):
        return dev(zl, h, x, 2 * zh + lax.div(y, 2), lax.rem(y, 2))

    def spread_from(h):
        return dev(y, lax.div(zl, 2), lax.rem(zl, 2) * 2 + c, x, h)

    owner = dev(y, lax.div(zl, 2), x, 2 * zh + lax.rem(zl, 2), c)
    owned_from = dev(y, lax.div(zl, 2), x, 2 * zh + lax.rem(zl, 2), c)

    def is_me(d):
        return jnp.logical_and(d[0] == row, d[1] == col)

    def rows(ref, start, count):
        return ref.at[pl.ds(pl.multiple_of(start, 8), count)]

    sent = []

    def send(src, dst, sem, device, when=None):
        copy = pltpu.make_async_remote_copy(
            src_ref=src, dst_ref=dst, send_sem=send_sem.at[len(sent)], recv_sem=sem,
            device_id=device, device_id_type=MESH,
        )
        if when is None:
            copy.start()
        else:

            @pl.when(when)
            def _():
                copy.start()

        sent.append((copy, when))

    def send_or_keep(src, dst, sem, device):
        mine = is_me(device)
        copy = pltpu.make_async_remote_copy(
            src_ref=src, dst_ref=dst, send_sem=send_sem.at[len(sent)], recv_sem=sem,
            device_id=device, device_id_type=MESH,
        )
        keep = pltpu.make_async_copy(src, dst, sem)

        @pl.when(mine)
        def _():
            keep.start()

        @pl.when(jnp.logical_not(mine))
        def _():
            copy.start()

        sent.append((copy, jnp.logical_not(mine)))

    def finish():
        for copy, when in sent:
            if when is None:
                copy.wait_send()
            else:

                @pl.when(when)
                def _(copy=copy):
                    copy.wait_send()

    def arrived(dst, sem):
        pltpu.make_async_copy(dst, dst, sem).wait()

    load_a = pltpu.make_async_copy(mat, a, load_sem.at[0])
    load_t = pltpu.make_async_copy(tf, tfv, load_sem.at[3])
    load_v = [
        pltpu.make_async_copy(
            vec.at[p],
            vi.at[pl.ds(pl.multiple_of(col * 64, 8), 64), pl.ds(128 * p, 128)],
            load_sem.at[1 + p],
        )
        for p in range(2)
    ]
    for copy in load_v:
        copy.start()
    load_a.start()
    load_t.start()

    barrier = pltpu.get_barrier_semaphore()
    peers = [partner] + [at_x(k) for k in (1, 2, 3)] + [at_y(k) for k in (1, 2, 3)]
    peers += [at_z(k) for k in range(1, 8)]
    for peer in peers:
        pl.semaphore_signal(barrier, inc=1, device_id=peer, device_id_type=MESH)
    others = [f(h) for f in (spread_to, spread_from) for h in range(2)] + [owner, owned_from]
    for peer in others:

        @pl.when(jnp.logical_not(is_me(peer)))
        def _(peer=peer):
            pl.semaphore_signal(barrier, inc=1, device_id=peer, device_id_type=MESH)

    for copy in load_v:
        copy.wait()
    count = len(peers) + len(others)
    for peer in others:
        count = count - is_me(peer).astype(jnp.int32)
    pl.semaphore_wait(barrier, count)

    class Gather:
        def __init__(self, n, big, place):
            self.n, self.big, self.place = n, big, place

        def blk(self, y_, zl_, c_):
            return rows(self.big, self.place(y_, zl_, c_) * 64, 64)

        def half(self, y_, zl_, c_, h):
            return rows(self.big, self.place(y_, zl_, c_) * 64 + 32 * h, 32)

        def to_partner(self, n, k):
            b = self.blk(yn[n], zk[k], c)
            send(b, b, cr.at[self.n, n, k], partner)

        def to_y(self, k):
            if k in DIRECT:
                b = self.blk(y, zk[k], c)
                for s, n in ((0, 1), (2, 3), (4, 2)):
                    send(b, b, yr.at[self.n, k, s], at_y(n))
                return
            for h, s in ((0, 0), (1, 1)):
                b = self.half(y, zk[k], c, h)
                send(b, b, yr.at[self.n, k, s], at_y(1))
            for h, s in ((1, 2), (0, 3)):
                b = self.half(y, zk[k], c, h)
                send(b, b, yr.at[self.n, k, s], at_y(3))

        def to_z(self, k, n, h, when):
            b = self.half(y, zk[k], c, h)
            sem = {(0, 1): 0, (0, 2): 1, (1, 2): 2, (2, 1): 1, (3, 1): 2}[k, n]
            send(b, b, zr.at[self.n, sem, h], at_zl(n), when)

        def start(self):
            for h in range(2):
                self.to_z(0, 1, h, None)
                self.to_z(0, 2, h, middle)
            self.to_y(0)
            self.to_partner(0, 0)

        def z_step(self, k):
            for h in range(2):
                arrived(self.half(y, zk[k], c, h), zr.at[self.n, k - 1, h])
                self.to_z(k, 2 if k == 1 else 1, h, middle)
            self.to_y(k)
            self.to_partner(0, k)

        def y_step(self, k):
            if k in DIRECT:
                for n, s in ((1, 0), (2, 2)):
                    arrived(self.blk(yn[n], zk[k], c), yr.at[self.n, k, s])
                    self.to_partner(n, k)
                return
            for n, h, s, to in ((1, 0, 0, 1), (2, 1, 2, 3)):
                b = self.half(yn[n], zk[k], c, h)
                arrived(b, yr.at[self.n, k, s])
                send(b, b, yr.at[self.n, k, 4 + h], at_y(to))
            for n, h, s in ((1, 1, 1), (2, 0, 3)):
                arrived(self.half(yn[n], zk[k], c, h), yr.at[self.n, k, s])
                self.to_partner(n, k)

        def y_last(self, k):
            if k in DIRECT:
                arrived(self.blk(yn[3], zk[k], c), yr.at[self.n, k, 4])
                self.to_partner(3, k)
                return
            for h in range(2):
                arrived(self.half(yn[3], zk[k], c, h), yr.at[self.n, k, 4 + h])
            self.to_partner(3, k)

        def from_partner(self, n):
            for k in range(4):
                arrived(self.blk(yn[n], zk[k], 1 - c), cr.at[self.n, n, k])

    class Ring:
        def __init__(self, n, small):
            self.n, self.small = n, small

        def own(self, k):
            return rows(self.small, mod4(x + k) * 128, 128)

        def start(self):
            for k in (1, 3, 2):
                send(self.own(0), self.own(0), xr.at[self.n, k - 1], at_x(k))

        def last(self):
            for k in (1, 3, 2):
                arrived(self.own(-k), xr.at[self.n, k - 1])

    class Sum:
        def __init__(self, at, piece, buf, sem):
            self.at, self.piece, self.buf, self.sem = at, piece, buf, sem

        def first(self):
            send(self.piece(2, 0), self.buf(0), self.sem(0), self.at(1))
            send(self.piece(2, 1), self.buf(1), self.sem(1), self.at(3))
            send(self.piece(1, 1), self.buf(2), self.sem(2), self.at(1))
            send(self.piece(3, 0), self.buf(3), self.sem(3), self.at(3))

        def second(self):
            for h, k, to in ((0, 1, 1), (1, 3, 3)):
                arrived(self.buf(h), self.sem(h))
                self.buf(6 + h)[...] = self.buf(h)[...] + self.piece(k, h)[...]
                send(self.buf(6 + h), self.buf(4 + h), self.sem(4 + h), self.at(to))

        def last(self, out):
            for h in range(2):
                arrived(self.buf(3 - h), self.sem(3 - h))
                arrived(self.buf(4 + h), self.sem(4 + h))
                out(h)[...] = self.piece(0, h)[...] + (self.buf(4 + h)[...] + self.buf(3 - h)[...])

    gv = Gather(0, vi, lambda y_, zl_, c_: (y_ * 4 + zl_) * 2 + c_)
    rv = Ring(0, vj)
    gv.start()
    for h in range(2):
        send_or_keep(
            gv.blk(y, zl, c), rows(vj, (2 * zl + c) * 64, 64), l2r.at[c], spread_to(h)
        )
    for k in (1, 2, 3):
        gv.z_step(k)
    for k in range(3):
        gv.y_step(k)
    for h in range(2):
        arrived(rows(vj, (2 * x + h) * 64, 64), l2r.at[h])
    rv.start()
    gv.y_step(3)
    load_a.wait()
    load_t.wait()

    def chunk(n):
        start = pl.multiple_of(yn[n] * 512, 512)
        vt = vi[pl.ds(start, 512), :].T
        return dot3(split(vt), split(a[pl.ds(start, 512), :]))

    gv.from_partner(0)
    pt = chunk(0)
    for k in range(4):
        gv.y_last(k)
    gv.from_partner(1)
    pt += chunk(1)
    gv.from_partner(2)
    pt += chunk(2)
    gv.from_partner(3)
    pt += chunk(3)
    part[...] = pt.T

    xsum = Sum(
        at_x,
        lambda m, h: rows(part, mod4(x + m) * 128 + 64 * h, 64),
        lambda m: xb.at[m],
        lambda m: rsr.at[m],
    )
    xsum.first()

    rv.last()
    sp_[...] = dot3(split(vj[...].T), split(part[...]))
    own = gv.blk(y, zl, c)[...]
    sp_[128:256, 0:128] = dot3(split(own[:, :128].T), split(own[:, 128:]))
    send(rows(sp_, 128 * (1 - c), 128), s1, s1r, partner)
    xsum.second()
    arrived(s1, s1r)
    s128[...] = rows(sp_, 128 * c, 128)[...] + s1[...]
    for k in (1, 2, 3):
        send(rows(s128, 32 * mod4(x + k), 32), sx.at[k - 1], sxr.at[k - 1], at_x(k))

    xsum.last(lambda h: total.at[pl.ds(64 * h, 64)])
    send(rows(total, 64 * (1 - zh), 64), hx, hr.at[0], at_z(4))
    for k in range(3):
        arrived(sx.at[k], sxr.at[k])
    s32[...] = rows(s128, 32 * x, 32)[...] + sx[0] + (sx[1] + sx[2])
    for k in (1, 2, 3):
        send(rows(s32, 8 * mod4(y + k), 8), sy.at[k - 1], syr.at[k - 1], at_y(k))
    for k in range(3):
        arrived(sy.at[k], syr.at[k])
    s8[...] = rows(s32, 8 * y, 8)[...] + sy[0] + (sy[1] + sy[2])
    for k in range(1, 8):
        send(s8, sz.at[k - 1], szr.at[k - 1], at_z(k))
    arrived(hx, hr.at[0])
    p_own = rows(pj, x * 128 + 64 * zh, 64)
    p_own[...] = rows(total, 64 * zh, 64)[...] + hx[...]
    gp = Gather(
        1, pi, lambda y_, zl_, c_: (lax.rem(zl_, 2) * 2 + c_) * 8 + 2 * y_ + lax.div(zl_, 2)
    )
    send_or_keep(p_own, gp.blk(x, 2 * zh + lax.rem(zl, 2), c), l1r, owner)
    send(p_own, p_own, hr.at[1], at_z(4))

    def srow(x_, y_, c_):
        return rows(sfull, 128 * c_ + 32 * x_ + 8 * y_, 8)

    for k in range(7):
        arrived(sz.at[k], szr.at[k])
    srow(x, y, c)[...] = s8[...] + sz[0] + (sz[1] + sz[2]) + ((sz[3] + sz[4]) + (sz[5] + sz[6]))
    for k in (1, 2, 3):
        send(srow(x, y, c), srow(x, y, c), s4r.at[k - 1], at_y(k))
    arrived(gp.blk(y, zl, c), l1r)
    gp.start()
    for k in (1, 2, 3):
        arrived(srow(x, mod4(y - k), c), s4r.at[k - 1])
    s_own = rows(sfull, 128 * c + 32 * x, 32)
    for k in (1, 2, 3):
        send(s_own, s_own, s5r.at[k - 1], at_x(k))
    send(s_own, s_own, s6r.at[0], partner)
    rp = Ring(1, pj)
    arrived(rows(pj, x * 128 + 64 * (1 - zh), 64), hr.at[1])
    rp.start()
    gp.z_step(1)
    gp.z_step(2)
    gp.z_step(3)
    for k in (1, 2, 3):
        s_k = rows(sfull, 128 * c + 32 * mod4(x - k), 32)
        arrived(s_k, s5r.at[k - 1])
        send(s_k, s_k, s6r.at[k], partner)
    gp.y_step(0)
    for k in range(4):
        arrived(rows(sfull, 128 * (1 - c) + 32 * mod4(x - k), 32), s6r.at[k])

    upper = lax.broadcasted_iota(jnp.int32, (128, 128), 0) <= lax.broadcasted_iota(
        jnp.int32, (128, 128), 1
    )
    t1 = jnp.where(upper, tfv[0], 0.0)
    t2 = jnp.where(upper, tfv[1], 0.0)
    s11, s12 = sfull[0:128, 0:128], sfull[0:128, 128:256]
    n12, s22 = sfull[128:256, 0:128], sfull[128:256, 128:256]
    t1t, t2t = t1.T, t2.T
    b = dot_full(t1t, dot_full(s11, t1))
    e = dot_full(t1t, s12)
    nt2 = dot_full(n12, t2)
    gp.y_step(1)
    h = dot_full(b.T, n12)
    k12 = dot_full(h - e, t2)
    m12 = -dot_full(t1, nt2)
    f = dot_full(n12.T, e - 0.5 * h)
    gp.y_step(2)
    b2 = dot_full(t2t, dot_full(s22 - f - f.T, t2))
    zero = jnp.zeros((128, 128), F32)
    kk = jnp.concatenate(
        [
            jnp.concatenate([-0.5 * (b + b.T), k12], axis=1),
            jnp.concatenate([k12.T, -0.5 * (b2 + b2.T)], axis=1),
        ],
        axis=0,
    )
    mm = jnp.concatenate(
        [jnp.concatenate([t1, m12], axis=1), jnp.concatenate([zero, t2], axis=1)], axis=0
    )
    rp.last()
    v_s = split(vj[...])
    xj = dot3(split(pj[...]), split(mm)) + dot3(v_s, split(kk))
    x_s = split(xj.T)
    gp.y_step(3)
    zj = dot3(v_s, split(mm.T))
    zh_out[...], zl_out[...] = split(zj.T)
    for n in range(4):
        if n == 2:
            for k in range(4):
                gp.y_last(k)
        r = slice(512 * n, 512 * n + 512)
        a2[r, :] = a[r, :] - dot3(split(vi[r, :]), x_s)
    for n in range(4):
        gp.from_partner(n)
    finish()


def exchange(matrix, vectors, tfactor):
    def vmem(*shape):
        return pltpu.VMEM(shape, F32)

    def dma(*shape):
        return pltpu.SemaphoreType.DMA(shape)

    return pl.pallas_call(
        exchange_kernel,
        out_shape=(
            jax.ShapeDtypeStruct((2048, 512), F32),
            jax.ShapeDtypeStruct((2048, 256), F32),
            jax.ShapeDtypeStruct((256, 512), BF16),
            jax.ShapeDtypeStruct((256, 512), BF16),
        ),
        in_specs=[pl.BlockSpec(memory_space=pltpu.HBM)] * 3,
        out_specs=(pl.BlockSpec(memory_space=pltpu.VMEM),) * 4,
        scratch_shapes=[
            vmem(2048, 512), vmem(2048, 256), vmem(512, 256), vmem(512, 256), vmem(512, 256),
            vmem(8, 64, 256), vmem(128, 256), vmem(64, 256),
            vmem(256, 256), vmem(128, 256), vmem(128, 256), vmem(3, 32, 256), vmem(32, 256),
            vmem(3, 8, 256), vmem(8, 256), vmem(7, 8, 256), vmem(256, 256), vmem(2, 128, 128),
            dma(160), dma(4), dma(2, 3, 2), dma(2, 4, 6), dma(2, 4, 4), dma(2), dma(2, 6),
            dma(6), dma(), dma(2), dma(), dma(3), dma(3), dma(7), dma(3), dma(3), dma(4),
        ],
        compiler_params=pltpu.CompilerParams(
            collective_id=0, has_side_effects=True, vmem_limit_bytes=36 << 20
        ),
    )(*(pltpu.with_memory_space_constraint(v, pltpu.HBM) for v in (matrix, vectors, tfactor)))


def update_kernel(mat, pi, zh, zl, out):
    out[...] = mat[...] - dot3(split(pi[...]), (zh[...], zl[...]))


def update(matrix, pi, zh, zl):
    rows_here, cols_here = matrix.shape
    step = 1024
    return pl.pallas_call(
        update_kernel,
        grid=(rows_here // step,),
        out_shape=jax.ShapeDtypeStruct(matrix.shape, F32),
        in_specs=[
            pl.BlockSpec((step, cols_here), lambda i: (i, 0)),
            pl.BlockSpec((step, 256), lambda i: (i, 0)),
            pl.BlockSpec((256, 512), lambda i: (0, 0)),
            pl.BlockSpec((256, 512), lambda i: (0, 0)),
        ],
        out_specs=pl.BlockSpec((step, cols_here), lambda i: (i, 0)),
        compiler_params=pltpu.CompilerParams(vmem_limit_bytes=20 << 20),
    )(matrix, pi, zh, zl)


def body(matrix, vectors, tfactor):
    return update(*exchange(matrix, vectors, tfactor))


def solution(mesh):
    return jax.shard_map(
        body,
        mesh=mesh,
        in_specs=(P("row", "col"), P(None, ("row", "col"), None), P()),
        out_specs=P("row", "col"),
        check_vma=False,
    )
```
